768 devices in a mesh: lon: 96 (over x, y_hi, z), lat: 8 (over y_lo, core).
Axes of the slice: x: 4, y: 8 (y_hi: 2, y_lo: 4; y = y_hi * 4 + y_lo), z: 12, core: 2. Of those that a mesh axis runs over, the one named last changes fastest.
Arguments:
- fields: bfloat16 [256, 4608, 128], P('lat', 'lon'), may hold values from -6 to 6
- ocean: int32 [256, 4608], P('lat', 'lon'), may hold values 0 or 1
- cotangent: bfloat16 [256, 4608, 128], P('lat', 'lon'), may hold values from -6 to 6
- kernel: float32 [7, 7, 128], replicated, may hold values from -0.875 to 0.875
- ln_gain: float32 [128], replicated, may hold values from 0.1 to 1.9
- w_in: bfloat16 [128, 256], replicated, may hold values from -0.5 to 0.5
- b_in: float32 [256], replicated, may hold values from -3 to 3
- w_out: bfloat16 [256, 128], replicated, may hold values from -0.375 to 0.375
Outputs:
- advanced: bfloat16 [256, 4608, 128], P('lat', 'lon')
- field_grad: bfloat16 [256, 4608, 128], P('lat', 'lon')
- kernel_grad: float32 [7, 7, 128], replicated
- w_in_grad: float32 [128, 256], replicated
- w_out_grad: float32 [256, 128], replicated
The draws below stay inside these ranges and needn't reach their ends.
Inputs may be any that keep to these rules, and one draw needn't show every extreme that they name: 1 marks an ocean cell, 0 a land cell.
All inputs are finite; a program needn't handle non-finite values. No bound on the sum of `ocean` on one device may be relied on, other than what follows from the above.
Results may differ from the reference program's by a relative error of at most 0.0056.
Values may be sent and summed in bfloat16 or wider, within the bound.
No kernel may reach another device: no remote copies, remote signals or barrier semaphores. Data moves between devices by JAX's collectives and lax.ppermute only.
A program may use at most 32 MiB of HBM per device.

```python
import jax
import jax.numpy as jnp
from jax import lax

C = 128
FF = 256
KS = 7
LAT_DEV = 32
LON_DEV = 48
LAT = 256
LON = 4608
N_LON = 96
N_LAT = 8


def set_ends(drawn, own_key, smallest, high):
    extent = drawn.shape
    spot = [jax.random.randint(jax.random.fold_in(own_key, axis), (), 0, extent[axis]) for axis in range(len(extent))]
    drawn = drawn.at[tuple(spot)].set(smallest)
    longest = extent.index(max(extent))
    spot[longest] = (spot[longest] + 1) % extent[longest]
    return drawn.at[tuple(spot)].set(high)


def level_of(stream_key, extent, split, low, largest):
    factor_of = 1.0
    for dim, parts in split:
        heights = jax.random.uniform(jax.random.fold_in(jax.random.fold_in(stream_key, 6), dim), (parts,), jnp.float32, low / len(split), largest / len(split))
        factor_of = factor_of * jnp.repeat(jnp.exp(heights), extent[dim] // parts).reshape((-1,) + (1,) * (len(extent) - 1 - dim))
    return factor_of


def centred(own_key, dims, spread, most, cuts=(), kind=jnp.bfloat16):
    entries = jax.random.normal(own_key, dims, jnp.float32) * spread
    if len(cuts) > 0:
        entries = level_of(own_key, dims, cuts, -0.22, 0.18) * entries
    return jnp.clip(entries, min=-most, max=most).astype(kind)


def setup_inputs(seed: int = 0) -> dict:
    seeds = jax.random.split(jax.random.key(seed), 9)
    fields = centred(seeds[0], (LAT, LON, C), 1.0, 6.0, ((0, 8), (1, 96)))
    ocean = set_ends((jax.random.randint(seeds[1], (LAT, LON), 0, 10) < 7).astype(jnp.int32), jax.random.fold_in(seeds[1], 1), 0, 1)
    cotangent = centred(seeds[2], (LAT, LON, C), 1.0, 6.0, ((0, 8), (1, 96)))
    kernel = centred(seeds[3], (KS, KS, C), (KS * KS) ** -0.5, 0.875, (), jnp.float32)
    ln_gain = jnp.clip(1.0 + 0.18 * jax.random.normal(seeds[4], (C,), jnp.float32), 0.1, 1.9)
    w_in = centred(seeds[5], (C, FF), C ** -0.5, 0.5)
    b_in = centred(seeds[6], (FF,), 0.5, 3.0, (), jnp.float32)
    w_out = centred(seeds[7], (FF, C), FF ** -0.5, 0.375)
    return dict(fields=fields, ocean=ocean, cotangent=cotangent, kernel=kernel, ln_gain=ln_gain, w_in=w_in, b_in=b_in, w_out=w_out)


def depthwise(padded, kernel, row_count, col_count):
    running = jnp.zeros((row_count, col_count, padded.shape[2]), jnp.float32)
    for row_off in range(7):
        for col_off in range(7):
            running = running + padded[row_off:row_off + row_count, col_off:col_off + col_count].astype(jnp.float32) * kernel[row_off, col_off]
    return running

def depthwise_back(padded, kernel, row_count, col_count):
    running = jnp.zeros((row_count, col_count, padded.shape[2]), jnp.float32)
    for row_off in range(7):
        for col_off in range(7):
            running = running + padded[6 - row_off:6 - row_off + row_count, 6 - col_off:6 - col_off + col_count].astype(jnp.float32) * kernel[row_off, col_off]
    return running

def kernel_terms(padded, dz_cells, row_count, col_count):
    grads = dz_cells.astype(jnp.float32)
    rows_out = []
    for row_off in range(7):
        line = []
        for col_off in range(7):
            line.append(lax.optimization_barrier(jnp.sum(padded[row_off:row_off + row_count, col_off:col_off + col_count].astype(jnp.float32) * grads, axis=(0, 1))))
        rows_out.append(jnp.stack(line))
    return jnp.stack(rows_out)

def pointwise(z_cells, gmask, ln_gain, w_in, b_in, w_out, inner):
    grid_shape = z_cells.shape
    flat_cells = z_cells.reshape(-1, grid_shape[-1])
    flat_grad = gmask.reshape(-1, grid_shape[-1])
    average = lax.optimization_barrier(jnp.mean(flat_cells, axis=-1, keepdims=True))
    centre = flat_cells - average
    inverse = lax.rsqrt(lax.optimization_barrier(jnp.mean(centre * centre, axis=-1, keepdims=True)) + 1e-06)
    unit_cells = centre * inverse
    normed = (unit_cells * ln_gain).astype(jnp.bfloat16)
    preact = jnp.dot(normed, w_in, preferred_element_type=jnp.float32) + b_in
    normal_cdf = 0.5 * (1.0 + lax.erf(preact * 0.7071067811865476))
    hidden = (preact * normal_cdf).astype(jnp.bfloat16)
    out_term = jnp.dot(hidden, w_out, preferred_element_type=jnp.float32)
    d_hidden = lax.dot_general(flat_grad, w_out, (((1,), (1,)), ((), ())), preferred_element_type=jnp.float32)
    slopes = normal_cdf + preact * jnp.exp(-0.5 * preact * preact) * 0.3989422804014327
    d_pre = (d_hidden * slopes).astype(jnp.bfloat16)
    if inner is None:
        grad_used = flat_grad
        pre_used = d_pre
    else:
        grad_used = flat_grad * inner
        pre_used = d_pre * inner
    w_out_term = lax.dot_general(hidden, grad_used, (((0,), (0,)), ((), ())), preferred_element_type=jnp.float32)
    w_in_term = lax.dot_general(normed, pre_used, (((0,), (0,)), ((), ())), preferred_element_type=jnp.float32)
    d_norm = lax.dot_general(d_pre, w_in, (((1,), (1,)), ((), ())), preferred_element_type=jnp.float32)
    scaled = d_norm * ln_gain
    dz_flat = inverse * (scaled - lax.optimization_barrier(jnp.mean(scaled, axis=-1, keepdims=True)) - unit_cells * lax.optimization_barrier(jnp.mean(scaled * unit_cells, axis=-1, keepdims=True)))
    return (out_term.reshape(grid_shape), dz_flat.astype(jnp.bfloat16).reshape(grid_shape), w_in_term, w_out_term)

def pad_grid(values, width):
    wrapped = jnp.concatenate([values[:, -width:], values, values[:, :width]], axis=1)
    return jnp.pad(wrapped, ((width, width), (0, 0), (0, 0)))

def reference(fields, ocean, cotangent, kernel, ln_gain, w_in, b_in, w_out):
    ocean_b = ocean.astype(jnp.bfloat16)[..., None]
    ocean_f = ocean.astype(jnp.float32)[..., None]
    masked = fields * ocean_b
    gmask = cotangent * ocean_b
    padded = pad_grid(masked, 3)
    width = padded.shape[1] - 6

    def forward(block):
        start = (block * LAT_DEV).astype(jnp.int32)
        slab = lax.dynamic_slice_in_dim(padded, start, LAT_DEV + 6, 0)
        z_cells = depthwise(slab, kernel, LAT_DEV, width)
        grads = lax.dynamic_slice_in_dim(gmask, start, LAT_DEV, 0)
        out_term, dz_cells, w_in_term, w_out_term = pointwise(z_cells, grads, ln_gain, w_in, b_in, w_out, None)
        base = lax.dynamic_slice_in_dim(fields, start, LAT_DEV, 0).astype(jnp.float32)
        keep = lax.dynamic_slice_in_dim(ocean_f, start, LAT_DEV, 0)
        advanced = (keep * (base + out_term)).astype(jnp.bfloat16)
        return (advanced, dz_cells, kernel_terms(slab, dz_cells, LAT_DEV, width), w_in_term, w_out_term)
    blocks = jnp.arange(N_LAT, dtype=jnp.int32)
    advanced, dz_all, kernel_part, w_in_part, w_out_part = lax.map(forward, blocks)
    advanced = advanced.reshape(fields.shape)
    dz_all = dz_all.reshape(fields.shape)
    dz_padded = pad_grid(dz_all, 3)

    def backward(block):
        start = (block * LAT_DEV).astype(jnp.int32)
        slab = lax.dynamic_slice_in_dim(dz_padded, start, LAT_DEV + 6, 0)
        back = depthwise_back(slab, kernel, LAT_DEV, width)
        keep = lax.dynamic_slice_in_dim(ocean_f, start, LAT_DEV, 0)
        incoming = lax.dynamic_slice_in_dim(cotangent, start, LAT_DEV, 0).astype(jnp.float32)
        return (keep * (incoming + back)).astype(jnp.bfloat16)
    field_grad = lax.map(backward, blocks).reshape(fields.shape)
    factor = 1.0 / jnp.sqrt(jnp.float32(LAT_DEV * LON_DEV * N_LAT * N_LON))
    kernel_grad = lax.optimization_barrier(jnp.sum(kernel_part, axis=0)) * factor
    w_in_grad = lax.optimization_barrier(jnp.sum(w_in_part, axis=0)) * factor
    w_out_grad = lax.optimization_barrier(jnp.sum(w_out_part, axis=0)) * factor
    return (advanced, field_grad, kernel_grad, w_in_grad, w_out_grad)
```

```python
import jax
import jax.numpy as jnp
from jax import lax
from jax.sharding import Mesh
from jax.sharding import PartitionSpec as P

LINK = jnp.bfloat16
LON = ("x", "yh", "z")
LAT = ("yl", "core")
OUTER = ("x", "yh", "yl", "core")
INNER = ("z",)


def with_halo(cells, sides, width):
    for axis, dim in sides:
        count = lax.axis_size(axis)
        head = lax.slice_in_dim(cells, 0, width, axis=dim)
        tail = lax.slice_in_dim(cells, cells.shape[dim] - width, cells.shape[dim], axis=dim)
        cells = jnp.concatenate(
            [
                lax.ppermute(tail, axis, [(i, (i + 1) % count) for i in range(count)]),
                cells,
                lax.ppermute(head, axis, [((i + 1) % count, i) for i in range(count)]),
            ],
            axis=dim,
        )
    return cells


def depthwise(padded, kernel, row_count, col_count):
    running = jnp.zeros((row_count, col_count, padded.shape[2]), jnp.float32)
    for row_off in range(7):
        for col_off in range(7):
            running = (
                running
                + padded[row_off : row_off + row_count, col_off : col_off + col_count].astype(
                    jnp.float32
                )
                * kernel[row_off, col_off]
            )
    return running


def depthwise_back(padded, kernel, row_count, col_count):
    running = jnp.zeros((row_count, col_count, padded.shape[2]), jnp.float32)
    for row_off in range(7):
        for col_off in range(7):
            running = (
                running
                + padded[
                    6 - row_off : 6 - row_off + row_count, 6 - col_off : 6 - col_off + col_count
                ].astype(jnp.float32)
                * kernel[row_off, col_off]
            )
    return running


def kernel_terms(padded, dz_cells, row_count, col_count):
    grads = dz_cells.astype(jnp.float32)
    rows_out = []
    for row_off in range(7):
        line = []
        for col_off in range(7):
            line.append(
                jnp.sum(
                    padded[row_off : row_off + row_count, col_off : col_off + col_count].astype(
                        jnp.float32
                    )
                    * grads,
                    axis=(0, 1),
                )
            )
        rows_out.append(jnp.stack(line))
    return jnp.stack(rows_out)


def pointwise(z_cells, gmask, ln_gain, w_in, b_in, w_out):
    grid_shape = z_cells.shape
    flat_cells = z_cells.reshape(-1, grid_shape[-1])
    flat_grad = gmask.reshape(-1, grid_shape[-1])
    average = jnp.mean(flat_cells, axis=-1, keepdims=True)
    centre = flat_cells - average
    inverse = lax.rsqrt(jnp.mean(centre * centre, axis=-1, keepdims=True) + 1e-06)
    unit_cells = centre * inverse
    normed = (unit_cells * ln_gain).astype(jnp.bfloat16)
    preact = jnp.dot(normed, w_in, preferred_element_type=jnp.float32) + b_in
    normal_cdf = 0.5 * (1.0 + lax.erf(preact * 0.7071067811865476))
    hidden = (preact * normal_cdf).astype(jnp.bfloat16)
    out_term = jnp.dot(hidden, w_out, preferred_element_type=jnp.float32)
    d_hidden = lax.dot_general(
        flat_grad, w_out, (((1,), (1,)), ((), ())), preferred_element_type=jnp.float32
    )
    slopes = normal_cdf + preact * jnp.exp(-0.5 * preact * preact) * 0.3989422804014327
    d_pre = (d_hidden * slopes).astype(jnp.bfloat16)
    w_out_term = lax.dot_general(
        hidden, flat_grad, (((0,), (0,)), ((), ())), preferred_element_type=jnp.float32
    )
    w_in_term = lax.dot_general(
        normed, d_pre, (((0,), (0,)), ((), ())), preferred_element_type=jnp.float32
    )
    d_norm = lax.dot_general(
        d_pre, w_in, (((1,), (1,)), ((), ())), preferred_element_type=jnp.float32
    )
    scaled = d_norm * ln_gain
    dz_flat = inverse * (
        scaled
        - jnp.mean(scaled, axis=-1, keepdims=True)
        - unit_cells * jnp.mean(scaled * unit_cells, axis=-1, keepdims=True)
    )
    return (
        out_term.reshape(grid_shape),
        dz_flat.astype(jnp.bfloat16).reshape(grid_shape),
        w_in_term,
        w_out_term,
    )


def zero_poles(padded, width):
    position = lax.axis_index(LAT)
    count = lax.axis_size(LAT)
    row_ids = lax.broadcasted_iota(jnp.int32, (padded.shape[0], 1, 1), 0)
    north = jnp.logical_and(position == 0, row_ids < width)
    south = jnp.logical_and(position == count - 1, row_ids >= padded.shape[0] - width)
    return jnp.where(jnp.logical_or(north, south), jnp.zeros_like(padded), padded)


def group_size(axes):
    size = 1
    for axis in axes:
        size *= lax.axis_size(axis)
    return size


def grid_sum(block):
    size = group_size(OUTER)
    chunk = block.shape[0] // size
    parts = lax.all_to_all(
        block.astype(LINK).reshape(size, chunk, 128), OUTER, 0, 0, tiled=True
    )
    own = jnp.sum(parts.astype(jnp.float32), axis=0)
    count = group_size(INNER)
    copies = jnp.broadcast_to(own[None], (count, chunk, 128))
    total = jnp.sum(lax.all_to_all(copies, INNER, 0, 0, tiled=True), axis=0)
    spread = jnp.broadcast_to(total.astype(LINK)[None], (size, chunk, 128))
    return lax.all_to_all(spread, OUTER, 0, 0, tiled=True).reshape(size * chunk, 128)


def sum_terms(kernel_term, w_in_term, w_out_term):
    block = jnp.concatenate(
        [
            w_in_term.reshape(-1, 128),
            w_out_term,
            kernel_term.reshape(49, 128),
            jnp.zeros((15, 128), jnp.float32),
        ]
    )
    total = grid_sum(block).astype(jnp.float32)
    return (
        total[512:561].reshape(7, 7, 128),
        total[0:256].reshape(128, 256),
        total[256:512],
    )


def shards(fields, ocean, cotangent, kernel, ln_gain, w_in, b_in, w_out):
    row_count = fields.shape[0]
    col_count = fields.shape[1]
    ocean_b = ocean.astype(jnp.bfloat16)[..., None]
    ocean_f = ocean.astype(jnp.float32)[..., None]
    masked = fields * ocean_b
    gmask = cotangent * ocean_b
    padded = zero_poles(with_halo(masked, ((LON, 1), (LAT, 0)), 3), 3)
    z_cells = depthwise(padded, kernel, row_count, col_count)
    out_term, dz_cells, w_in_term, w_out_term = pointwise(
        z_cells, gmask, ln_gain, w_in, b_in, w_out
    )
    kernel_term = kernel_terms(padded, dz_cells, row_count, col_count)
    dz_padded = zero_poles(with_halo(dz_cells, ((LON, 1), (LAT, 0)), 3), 3)
    advanced = (ocean_f * (fields.astype(jnp.float32) + out_term)).astype(jnp.bfloat16)
    back = depthwise_back(dz_padded, kernel, row_count, col_count)
    field_grad = (ocean_f * (cotangent.astype(jnp.float32) + back)).astype(jnp.bfloat16)
    kernel_sum, w_in_sum, w_out_sum = sum_terms(kernel_term, w_in_term, w_out_term)
    factor = 1.0 / jnp.sqrt(
        jnp.float32(row_count * col_count * lax.axis_size(LAT) * lax.axis_size(LON))
    )
    return (advanced, field_grad, kernel_sum * factor, w_in_sum * factor, w_out_sum * factor)


def solution(mesh):
    torus = Mesh(mesh.devices.reshape(4, 2, 12, 4, 2), LON + LAT)
    cells = P(LAT, LON, None)
    in_specs = (cells, P(LAT, LON), cells, P(), P(), P(), P(), P())
    out_specs = (cells, cells, P(), P(), P())
    return jax.shard_map(shards, mesh=torus, in_specs=in_specs, out_specs=out_specs, check_vma=False)
```

```python
import jax
import jax.numpy as jnp
from jax import lax
from jax.experimental import pallas as pl
from jax.experimental.pallas import tpu as pltpu
from jax.sharding import Mesh
from jax.sharding import PartitionSpec as P

LINK = jnp.bfloat16
LON = ("x", "yh", "z")
LAT = ("yl", "core")
OUTER = ("x", "yh", "yl", "core")
INNER = ("z",)
ROWS = 32
COLS = 48
C = 128
FF = 256
LEFT = 8
STEP = 4
TERM_ROWS = 576


def fill(pad, own, west, east, north, south):
    f32 = jnp.float32
    pad[3 : 3 + ROWS, LEFT : LEFT + COLS, :] = own[...].astype(f32)
    pad[3 : 3 + ROWS, LEFT - 3 : LEFT, :] = west[...].astype(f32)
    pad[3 : 3 + ROWS, LEFT + COLS : LEFT + COLS + 3, :] = east[...].astype(f32)
    pad[0:3, LEFT - 3 : LEFT + COLS + 3, :] = north[...].astype(f32)
    pad[3 + ROWS : 6 + ROWS, LEFT - 3 : LEFT + COLS + 3, :] = south[...].astype(f32)


def conv_rows(pad, taps, first, flip):
    sums = [jnp.zeros((COLS, C), jnp.float32) for _ in range(STEP)]
    for row in range(STEP + 6):
        for col in range(7):
            cells = pad[first + row, LEFT - 3 + col : LEFT - 3 + col + COLS, :]
            for out in range(STEP):
                tap = row - out
                if 0 <= tap < 7:
                    at = tap * 7 + col
                    at = 48 - at if flip else at
                    sums[out] = sums[out] + cells * taps[at : at + 1, :]
    return jnp.concatenate(sums, axis=0)


def main_kernel(
    masked, west, east, north, south, gmask, ocean, taps, gain, w_in, b_in, w_out,
    advanced, dz_out, terms, pad, acc_in, acc_out, acc_tap,
):
    f32, bf16 = jnp.float32, jnp.bfloat16
    fill(pad, masked, west, east, north, south)
    acc_in[...] = jnp.zeros_like(acc_in)
    acc_out[...] = jnp.zeros_like(acc_out)
    acc_tap[...] = jnp.zeros_like(acc_tap)
    size = STEP * COLS

    def block(step, carry):
        first = step * STEP
        z = conv_rows(pad, taps, first, False)
        grad = gmask[pl.ds(first, STEP)].reshape(size, C)
        average = jnp.mean(z, axis=-1, keepdims=True)
        centre = z - average
        inverse = lax.rsqrt(jnp.mean(centre * centre, axis=-1, keepdims=True) + 1e-06)
        unit = centre * inverse
        normed = (unit * gain[...]).astype(bf16)
        preact = jnp.dot(normed, w_in[...], preferred_element_type=f32) + b_in[...]
        cdf = 0.5 * (1.0 + lax.erf(preact * 0.7071067811865476))
        hidden = (preact * cdf).astype(bf16)
        out = jnp.dot(hidden, w_out[...], preferred_element_type=f32)
        d_hidden = lax.dot_general(grad, w_out[...], (((1,), (1,)), ((), ())), preferred_element_type=f32)
        slopes = cdf + preact * jnp.exp(-0.5 * preact * preact) * 0.3989422804014327
        d_pre = (d_hidden * slopes).astype(bf16)
        contract = (((0,), (0,)), ((), ()))
        acc_out[...] += lax.dot_general(grad, hidden, contract, preferred_element_type=f32)
        acc_in[...] += lax.dot_general(normed, d_pre, contract, preferred_element_type=f32)
        d_norm = lax.dot_general(d_pre, w_in[...], (((1,), (1,)), ((), ())), preferred_element_type=f32)
        scaled = d_norm * gain[...]
        dz = inverse * (
            scaled
            - jnp.mean(scaled, axis=-1, keepdims=True)
            - unit * jnp.mean(scaled * unit, axis=-1, keepdims=True)
        )
        dz = dz.astype(bf16)
        dz_out[pl.ds(first, STEP)] = dz.reshape(STEP, COLS, C)
        own = masked[pl.ds(first, STEP)].reshape(size, C).astype(f32)
        keep = ocean[pl.ds(first, STEP)].reshape(size, C).astype(f32)
        advanced[pl.ds(first, STEP)] = (own + keep * out).astype(bf16).reshape(STEP, COLS, C)
        grads = dz.astype(f32)
        for tap in range(7):
            for col in range(7):
                total = jnp.zeros((COLS, C), f32)
                for row in range(STEP):
                    cells = pad[first + row + tap, LEFT - 3 + col : LEFT - 3 + col + COLS, :]
                    total = total + cells * grads[row * COLS : (row + 1) * COLS]
                acc_tap[tap * 7 + col] += jnp.sum(total.reshape(COLS // 8, 8, C), axis=0)
        return carry

    lax.fori_loop(0, ROWS // STEP, block, 0)
    terms[0:C, :] = acc_in[:, 0:C].astype(LINK)
    terms[C : 2 * C, :] = acc_in[:, C:].astype(LINK)
    terms[2 * C : 2 * C + FF, :] = acc_out[...].T.astype(LINK)
    tap_sums = jnp.sum(acc_tap[...], axis=1)
    terms[512:576, :] = jnp.concatenate([tap_sums, jnp.zeros((15, C), f32)], axis=0).astype(LINK)


def back_kernel(dz, west, east, north, south, gmask, ocean, taps, field_grad, pad):
    f32 = jnp.float32
    fill(pad, dz, west, east, north, south)
    size = STEP * COLS

    def block(step, carry):
        first = step * STEP
        back = conv_rows(pad, taps, first, True)
        own = gmask[pl.ds(first, STEP)].reshape(size, C).astype(f32)
        keep = ocean[pl.ds(first, STEP)].reshape(size, C).astype(f32)
        field_grad[pl.ds(first, STEP)] = (own + keep * back).astype(jnp.bfloat16).reshape(STEP, COLS, C)
        return carry

    lax.fori_loop(0, ROWS // STEP, block, 0)


def call(body, args, outs, scratch, flops):
    vmem = pl.BlockSpec(memory_space=pltpu.VMEM)
    return pl.pallas_call(
        body,
        out_shape=outs,
        in_specs=[vmem] * len(args),
        out_specs=[vmem] * len(outs),
        scratch_shapes=scratch,
        compiler_params=pltpu.CompilerParams(vmem_limit_bytes=40 << 20),
        cost_estimate=pl.CostEstimate(flops=flops, bytes_accessed=2 << 20, transcendentals=1 << 19),
    )(*args)


def cells_type():
    return jax.ShapeDtypeStruct((ROWS, COLS, C), jnp.bfloat16)


def pad_type():
    return pltpu.VMEM((ROWS + 6, COLS + 16, C), jnp.float32)


def group_size(axes):
    size = 1
    for axis in axes:
        size *= lax.axis_size(axis)
    return size


def halo(cells):
    lon = group_size(LON)
    lat = group_size(LAT)
    west = lax.ppermute(cells[:, COLS - 3 :], LON, [(i, (i + 1) % lon) for i in range(lon)])
    east = lax.ppermute(cells[:, :3], LON, [((i + 1) % lon, i) for i in range(lon)])
    top = jnp.concatenate([west[:3], cells[:3], east[:3]], axis=1)
    bottom = jnp.concatenate([west[ROWS - 3 :], cells[ROWS - 3 :], east[ROWS - 3 :]], axis=1)
    north = lax.ppermute(bottom, LAT, [(i, i + 1) for i in range(lat - 1)])
    south = lax.ppermute(top, LAT, [(i + 1, i) for i in range(lat - 1)])
    return west, east, north, south


def grid_sum(block):
    size = group_size(OUTER)
    chunk = TERM_ROWS // size
    parts = lax.all_to_all(block.reshape(size, chunk, C), OUTER, 0, 0, tiled=True)
    own = jnp.sum(parts.astype(jnp.float32), axis=0)
    count = group_size(INNER)
    copies = jnp.broadcast_to(own[None], (count, chunk, C))
    total = jnp.sum(lax.all_to_all(copies, INNER, 0, 0, tiled=True), axis=0)
    spread = jnp.broadcast_to(total.astype(LINK)[None], (size, chunk, C))
    return lax.all_to_all(spread, OUTER, 0, 0, tiled=True).reshape(TERM_ROWS, C)


def shards(fields, ocean, cotangent, kernel, ln_gain, w_in, b_in, w_out):
    ocean_b = jnp.broadcast_to(ocean.astype(jnp.bfloat16)[..., None], fields.shape)
    masked = fields * ocean_b
    gmask = cotangent * ocean_b
    taps = kernel.reshape(49, C)
    advanced, dz, terms = call(
        main_kernel,
        (masked, *halo(masked), gmask, ocean_b, taps, ln_gain.reshape(1, C), w_in, b_in.reshape(1, FF), w_out),
        [cells_type(), cells_type(), jax.ShapeDtypeStruct((TERM_ROWS, C), LINK)],
        [
            pad_type(),
            pltpu.VMEM((C, FF), jnp.float32),
            pltpu.VMEM((C, FF), jnp.float32),
            pltpu.VMEM((49, 8, C), jnp.float32),
        ],
        500_000_000,
    )
    sums = grid_sum(terms).astype(jnp.float32)
    (field_grad,) = call(
        back_kernel, (dz, *halo(dz), gmask, ocean_b, taps), [cells_type()], [pad_type()], 20_000_000
    )
    factor = 1.0 / jnp.sqrt(
        jnp.float32(ROWS * COLS * group_size(LAT) * group_size(LON))
    )
    sums = sums * factor
    w_in_sum = jnp.concatenate([sums[:C], sums[C : 2 * C]], axis=1)
    return (advanced, field_grad, sums[512:561].reshape(7, 7, C), w_in_sum, sums[256:512])


def solution(mesh):
    torus = Mesh(mesh.devices.reshape(4, 2, 12, 4, 2), LON + LAT)
    cells = P(LAT, LON, None)
    in_specs = (cells, P(LAT, LON), cells, P(), P(), P(), P(), P())
    out_specs = (cells, cells, P(), P(), P())
    return jax.shard_map(shards, mesh=torus, in_specs=in_specs, out_specs=out_specs, check_vma=False)
```

```python
import functools

import jax
import jax.numpy as jnp
from jax import lax
from jax.experimental import pallas as pl
from jax.experimental.pallas import tpu as pltpu
from jax.sharding import Mesh
from jax.sharding import PartitionSpec as P

LINK = jnp.bfloat16
LON = ("x", "yh", "z")
LAT = ("yl", "core")
OUTER = ("x", "yh", "yl", "core")
INNER = ("z",)
ROWS = 32
COLS = 48
C = 128
FF = 256
TERM_ROWS = 576


INSIDE = ((8, 32),)
STRIPS = ((0, 8), (40, 8))


def fill_rows(pad, own, flags, halo_a, halo_b, first, last, at):
    f32 = jnp.float32
    even = flags[0] == 0
    pad[3 : 3 + ROWS, at : at + last - first, :] = own[:, first:last, :].astype(f32)
    from_a = halo_a[:, first:last, :].astype(f32)
    from_b = halo_b[:, first:last, :].astype(f32)
    pad[0:3, at : at + last - first, :] = jnp.where(even, from_b, from_a)
    pad[3 + ROWS : 6 + ROWS, at : at + last - first, :] = jnp.where(even, from_a, from_b)


def fill_strips(left, right, own, flags, lat_a, lat_b, lon_a, lon_b):
    f32 = jnp.float32
    even = flags[1] == 0
    fill_rows(left, own, flags, lat_a, lat_b, 0, 16, 8)
    fill_rows(right, own, flags, lat_a, lat_b, 32, 48, 0)
    from_a, from_b = lon_a[...].astype(f32), lon_b[...].astype(f32)
    left[:, 5:8, :] = jnp.where(even, from_b, from_a)
    right[:, 16:19, :] = jnp.where(even, from_a, from_b)


def conv_rows(pads, taps, first, step, flip):
    sums = [[jnp.zeros((width, C), jnp.float32) for _, _, width in pads] for _ in range(step)]
    for row in range(step + 6):
        for col in range(7):
            for seg, (pad, start, width) in enumerate(pads):
                cells = pad[first + row, start + col : start + col + width, :]
                for out in range(step):
                    tap = row - out
                    if 0 <= tap < 7:
                        at = tap * 7 + col
                        at = 48 - at if flip else at
                        sums[out][seg] = sums[out][seg] + cells * taps[at : at + 1, :]
    return jnp.concatenate([part for line in sums for part in line], axis=0)


def read_cells(ref, first, step, segs):
    return jnp.concatenate(
        [ref[first + row, c : c + w, :].astype(jnp.float32) for row in range(step) for c, w in segs], axis=0
    )


def write_cells(ref, first, step, segs, values):
    at = 0
    for row in range(step):
        for c, w in segs:
            ref[first + row, c : c + w, :] = values[at : at + w].astype(jnp.bfloat16)
            at += w


def main_rows(step, segs, pads, masked, gmask, ocean, params, advanced, dz_out, sums, index):
    f32, bf16 = jnp.float32, jnp.bfloat16
    taps, gain, w_in, b_in, w_out = params
    acc_in, acc_out, acc_tap = sums
    first = index * step
    z = conv_rows(pads, taps, first, step, False)
    grad = read_cells(gmask, first, step, segs).astype(bf16)
    average = jnp.mean(z, axis=-1, keepdims=True)
    centre = z - average
    inverse = lax.rsqrt(jnp.mean(centre * centre, axis=-1, keepdims=True) + 1e-06)
    unit = centre * inverse
    normed = (unit * gain[...]).astype(bf16)
    preact = jnp.dot(normed, w_in[...], preferred_element_type=f32) + b_in[...]
    cdf = 0.5 * (1.0 + lax.erf(preact * 0.7071067811865476))
    hidden = (preact * cdf).astype(bf16)
    out = jnp.dot(hidden, w_out[...], preferred_element_type=f32)
    d_hidden = lax.dot_general(grad, w_out[...], (((1,), (1,)), ((), ())), preferred_element_type=f32)
    slopes = cdf + preact * jnp.exp(-0.5 * preact * preact) * 0.3989422804014327
    d_pre = (d_hidden * slopes).astype(bf16)
    contract = (((0,), (0,)), ((), ()))
    acc_out[...] += lax.dot_general(grad, hidden, contract, preferred_element_type=f32)
    acc_in[...] += lax.dot_general(normed, d_pre, contract, preferred_element_type=f32)
    d_norm = lax.dot_general(d_pre, w_in[...], (((1,), (1,)), ((), ())), preferred_element_type=f32)
    scaled = d_norm * gain[...]
    dz = inverse * (
        scaled
        - jnp.mean(scaled, axis=-1, keepdims=True)
        - unit * jnp.mean(scaled * unit, axis=-1, keepdims=True)
    )
    write_cells(dz_out, first, step, segs, dz)
    own = read_cells(masked, first, step, segs)
    keep = read_cells(ocean, first, step, segs)
    write_cells(advanced, first, step, segs, own + keep * out)
    grads = dz.astype(bf16).astype(f32)
    per_row = sum(w for _, w in segs)
    for tap in range(7):
        for col in range(7):
            total = None
            for row in range(step):
                at = row * per_row
                for pad, start, width in pads:
                    cells = pad[first + row + tap, start + col : start + col + width, :]
                    product = cells * grads[at : at + width]
                    at += width
                    for part in range(0, width, 8):
                        piece = product[part : part + 8]
                        total = piece if total is None else total + piece
            acc_tap[tap * 7 + col] += total


def inside_kernel(
    flags, masked, lat_a, lat_b, gmask, ocean, taps, gain, w_in, b_in, w_out,
    advanced, dz_out, acc_in, acc_out, acc_tap, pad,
):
    fill_rows(pad, masked, flags, lat_a, lat_b, 0, COLS, 0)
    for acc in (acc_in, acc_out, acc_tap):
        acc[...] = jnp.zeros_like(acc)
    params = (taps, gain, w_in, b_in, w_out)

    def block(index, carry):
        main_rows(4, INSIDE, ((pad, 5, 32),), masked, gmask, ocean, params, advanced, dz_out, (acc_in, acc_out, acc_tap), index)
        return carry

    lax.fori_loop(0, ROWS // 4, block, 0)


def strips_kernel(
    flags, masked, lat_a, lat_b, lon_a, lon_b, gmask, ocean, taps, gain, w_in, b_in, w_out,
    had_advanced, had_dz, had_in, had_out, had_tap,
    advanced, dz_out, terms, left, right, acc_in, acc_out, acc_tap, lines,
):
    fill_strips(left, right, masked, flags, lat_a, lat_b, lon_a, lon_b)
    advanced[:, 8:40, :] = had_advanced[:, 8:40, :]
    dz_out[:, 8:40, :] = had_dz[:, 8:40, :]
    acc_in[...] = had_in[...]
    acc_out[...] = had_out[...]
    acc_tap[...] = had_tap[...]
    params = (taps, gain, w_in, b_in, w_out)

    def block(index, carry):
        main_rows(8, STRIPS, ((left, 5, 8), (right, 5, 8)), masked, gmask, ocean, params, advanced, dz_out, (acc_in, acc_out, acc_tap), index)
        return carry

    lax.fori_loop(0, ROWS // 8, block, 0)
    lines[0:C, :] = acc_in[:, 0:C]
    lines[C : 2 * C, :] = acc_in[:, C:]
    lines[2 * C : 2 * C + FF, :] = acc_out[...].T
    lines[512:561, :] = jnp.sum(acc_tap[...], axis=1)
    lines[561:576, :] = jnp.zeros((15, C), jnp.float32)
    chunk = terms.shape[1]
    for part in range(terms.shape[0]):
        terms[part] = lines[part * chunk : (part + 1) * chunk, :].astype(LINK)


def back_inside_kernel(flags, dz, lat_a, lat_b, gmask, ocean, taps, field_grad, pad):
    fill_rows(pad, dz, flags, lat_a, lat_b, 0, COLS, 0)

    def block(index, carry):
        back_rows(4, INSIDE, ((pad, 5, 32),), gmask, ocean, taps, field_grad, index)
        return carry

    lax.fori_loop(0, ROWS // 4, block, 0)


def back_strips_kernel(
    flags, dz, lat_a, lat_b, lon_a, lon_b, gmask, ocean, taps, had, field_grad, left, right
):
    fill_strips(left, right, dz, flags, lat_a, lat_b, lon_a, lon_b)
    field_grad[:, 8:40, :] = had[:, 8:40, :]

    def block(index, carry):
        back_rows(8, STRIPS, ((left, 5, 8), (right, 5, 8)), gmask, ocean, taps, field_grad, index)
        return carry

    lax.fori_loop(0, ROWS // 8, block, 0)


def back_rows(step, segs, pads, gmask, ocean, taps, field_grad, index):
    first = index * step
    back = conv_rows(pads, taps, first, step, True)
    own = read_cells(gmask, first, step, segs)
    keep = read_cells(ocean, first, step, segs)
    write_cells(field_grad, first, step, segs, own + keep * back)


def final_kernel(parts, kernel_grad, w_in_grad, w_out_grad, lines, *, factor):
    chunk = parts.shape[1]
    for part in range(parts.shape[0]):
        lines[part * chunk : (part + 1) * chunk, :] = parts[part].astype(jnp.float32) * factor
    w_in_grad[:, 0:C] = lines[0:C, :]
    w_in_grad[:, C:] = lines[C : 2 * C, :]
    w_out_grad[...] = lines[2 * C : 2 * C + FF, :]
    kernel_grad[...] = lines[512:561, :]


def call(body, args, outs, scratch, flops):
    vmem = pl.BlockSpec(memory_space=pltpu.VMEM)
    smem = pl.BlockSpec(memory_space=pltpu.SMEM)
    return pl.pallas_call(
        body,
        out_shape=outs,
        in_specs=[smem if a.dtype == jnp.int32 else vmem for a in args],
        out_specs=[vmem] * len(outs),
        scratch_shapes=scratch,
        compiler_params=pltpu.CompilerParams(vmem_limit_bytes=40 << 20),
        cost_estimate=pl.CostEstimate(flops=flops, bytes_accessed=2 << 20, transcendentals=1 << 19),
    )(*args)


def kind(*shape, dtype=jnp.float32):
    return jax.ShapeDtypeStruct(shape, dtype)


CELLS = kind(ROWS, COLS, C, dtype=jnp.bfloat16)
WIDE = pltpu.VMEM((ROWS + 6, COLS, C), jnp.float32)
NARROW = pltpu.VMEM((ROWS + 6, 24, C), jnp.float32)
SUMS = ((C, FF), (C, FF), (49, 8, C))


def group_size(axes):
    size = 1
    for axis in axes:
        size *= lax.axis_size(axis)
    return size


def exchange(low, high, axes, count, wraps):
    even = lax.axis_index(axes[-1]) % 2 == 0
    joins = [i for i in range(1, count, 2) if wraps or i + 1 < count]
    pairs_b = [(i, (i + 1) % count) for i in joins] + [((i + 1) % count, i) for i in joins]
    pairs_a = [(i, i + 1) for i in range(0, count, 2)] + [(i + 1, i) for i in range(0, count, 2)]
    from_b = lax.ppermute(jnp.where(even, low, high), axes, pairs_b)
    from_a = lax.ppermute(jnp.where(even, high, low), axes, pairs_a)
    return from_a, from_b


def lat_halo(top, bottom):
    return exchange(top, bottom, LAT, group_size(LAT), False)


def lon_halo(head, tail, lat_a, lat_b):
    even = lax.axis_index(LAT[-1]) % 2 == 0
    north = jnp.where(even, lat_b, lat_a)
    south = jnp.where(even, lat_a, lat_b)
    head = jnp.concatenate([north[:, :3], head, south[:, :3]])
    tail = jnp.concatenate([north[:, COLS - 3 :], tail, south[:, COLS - 3 :]])
    return exchange(head, tail, LON, group_size(LON), True)


def grid_sum(parts):
    size, chunk, _ = parts.shape
    parts = lax.all_to_all(parts, OUTER, 0, 0, tiled=True)
    own = jnp.sum(parts.astype(jnp.float32), axis=0)
    count = group_size(INNER)
    copies = jnp.broadcast_to(own[None], (count, chunk, C))
    total = jnp.sum(lax.all_to_all(copies, INNER, 0, 0, tiled=True), axis=0)
    spread = jnp.broadcast_to(total.astype(LINK)[None], (size, chunk, C))
    return lax.all_to_all(spread, OUTER, 0, 0, tiled=True)


def shards(fields, ocean, cotangent, kernel, ln_gain, w_in, b_in, w_out):
    flags = jnp.stack([lax.axis_index(LAT[-1]) % 2, lax.axis_index(LON[-1]) % 2]).astype(jnp.int32)
    taps = kernel.reshape(49, C)
    params = (taps, ln_gain.reshape(1, C), w_in, b_in.reshape(1, FF), w_out)

    def edge(rows, cols):
        return fields[rows, cols] * ocean[rows, cols].astype(jnp.bfloat16)[..., None]

    every = slice(None)
    top, bottom = edge(slice(0, 3), every), edge(slice(ROWS - 3, ROWS), every)
    head, tail = edge(every, slice(0, 3)), edge(every, slice(COLS - 3, COLS))
    lat = lat_halo(top, bottom)
    lon = lon_halo(head, tail, *lat)
    ocean_b = jnp.broadcast_to(ocean.astype(jnp.bfloat16)[..., None], fields.shape)
    masked = fields * ocean_b
    gmask = cotangent * ocean_b
    scratch = [pltpu.VMEM(shape, jnp.float32) for shape in SUMS]
    inside = call(
        inside_kernel,
        (flags, masked, *lat, gmask, ocean_b, *params),
        [CELLS, CELLS, *(kind(*shape) for shape in SUMS)],
        [WIDE],
        350_000_000,
    )
    parts = group_size(OUTER)
    advanced, dz, terms = call(
        strips_kernel,
        (flags, masked, *lat, *lon, gmask, ocean_b, *params, *inside),
        [CELLS, CELLS, kind(parts, TERM_ROWS // parts, C, dtype=LINK)],
        [NARROW, NARROW, *scratch, pltpu.VMEM((TERM_ROWS, C), jnp.float32)],
        170_000_000,
    )
    sums = grid_sum(terms)
    lat = lat_halo(dz[:3], dz[ROWS - 3 :])
    lon = lon_halo(dz[:, :3], dz[:, COLS - 3 :], *lat)
    (field_grad,) = call(
        back_inside_kernel, (flags, dz, *lat, gmask, ocean_b, taps), [CELLS], [WIDE], 100_000_000
    )
    (field_grad,) = call(
        back_strips_kernel,
        (flags, dz, *lat, *lon, gmask, ocean_b, taps, field_grad),
        [CELLS],
        [NARROW, NARROW],
        50_000_000,
    )
    cells = ROWS * COLS * group_size(LAT) * group_size(LON)
    kernel_grad, w_in_grad, w_out_grad = call(
        functools.partial(final_kernel, factor=cells**-0.5),
        (sums,),
        [kind(49, C), kind(C, FF), kind(FF, C)],
        [pltpu.VMEM((TERM_ROWS, C), jnp.float32)],
        1_000_000,
    )
    return (advanced, field_grad, kernel_grad.reshape(7, 7, C), w_in_grad, w_out_grad)


def solution(mesh):
    torus = Mesh(mesh.devices.reshape(4, 2, 12, 4, 2), LON + LAT)
    cells = P(LAT, LON, None)
    in_specs = (cells, P(LAT, LON), cells, P(), P(), P(), P(), P())
    out_specs = (cells, cells, P(), P(), P())
    return jax.shard_map(shards, mesh=torus, in_specs=in_specs, out_specs=out_specs, check_vma=False)
```

```python
import functools

import jax
import jax.numpy as jnp
from jax import lax
from jax.experimental import pallas as pl
from jax.experimental.pallas import tpu as pltpu
from jax.sharding import Mesh
from jax.sharding import PartitionSpec as P

LINK = jnp.bfloat16
LON = ("x", "yh", "z")
LAT = ("yl", "core")
OUTER = ("x", "yh", "yl", "core")
INNER = ("z",)
ROWS = 32
COLS = 48
C = 128
FF = 256
TERM_ROWS = 576


INSIDE = ((8, 32),)
STRIPS = ((0, 8), (40, 8))


def fill_rows(pad, own, flags, halo_a, halo_b, first, last, at):
    f32 = jnp.float32
    even = flags[0] == 0
    pad[3 : 3 + ROWS, at : at + last - first, :] = own[:, first:last, :].astype(f32)
    from_a = halo_a[:, first:last, :].astype(f32)
    from_b = halo_b[:, first:last, :].astype(f32)
    pad[0:3, at : at + last - first, :] = jnp.where(even, from_b, from_a)
    pad[3 + ROWS : 6 + ROWS, at : at + last - first, :] = jnp.where(even, from_a, from_b)


def fill_strips(left, right, own, flags, lat_a, lat_b, lon_a, lon_b):
    f32 = jnp.float32
    even = flags[1] == 0
    fill_rows(left, own, flags, lat_a, lat_b, 0, 16, 8)
    fill_rows(right, own, flags, lat_a, lat_b, 32, 48, 0)
    from_a, from_b = lon_a[...].astype(f32), lon_b[...].astype(f32)
    left[:, 5:8, :] = jnp.where(even, from_b, from_a)
    right[:, 16:19, :] = jnp.where(even, from_a, from_b)


def conv_rows(pads, taps, first, step, flip):
    sums = [[jnp.zeros((width, C), jnp.float32) for _, _, width in pads] for _ in range(step)]
    for row in range(step + 6):
        for col in range(7):
            for seg, (pad, start, width) in enumerate(pads):
                cells = pad[first + row, start + col : start + col + width, :]
                for out in range(step):
                    tap = row - out
                    if 0 <= tap < 7:
                        at = tap * 7 + col
                        at = 48 - at if flip else at
                        sums[out][seg] = sums[out][seg] + cells * taps[at : at + 1, :]
    return jnp.concatenate([part for line in sums for part in line], axis=0)


def read_cells(ref, first, step, segs):
    return jnp.concatenate(
        [ref[first + row, c : c + w, :].astype(jnp.float32) for row in range(step) for c, w in segs], axis=0
    )


def write_cells(ref, first, step, segs, values):
    at = 0
    for row in range(step):
        for c, w in segs:
            ref[first + row, c : c + w, :] = values[at : at + w].astype(jnp.bfloat16)
            at += w


def main_rows(step, segs, pads, masked, gmask, ocean, params, advanced, dz_out, sums, index):
    f32, bf16 = jnp.float32, jnp.bfloat16
    taps, gain, w_in, b_in, w_out = params
    acc_in, acc_out, acc_tap = sums
    first = index * step
    z = conv_rows(pads, taps, first, step, False)
    grad = read_cells(gmask, first, step, segs).astype(bf16)
    average = jnp.mean(z, axis=-1, keepdims=True)
    centre = z - average
    inverse = lax.rsqrt(jnp.mean(centre * centre, axis=-1, keepdims=True) + 1e-06)
    unit = centre * inverse
    normed = (unit * gain[...]).astype(bf16)
    preact = jnp.dot(normed, w_in[...], preferred_element_type=f32) + b_in[...]
    cdf = 0.5 * (1.0 + lax.erf(preact * 0.7071067811865476))
    hidden = (preact * cdf).astype(bf16)
    out = jnp.dot(hidden, w_out[...], preferred_element_type=f32)
    d_hidden = lax.dot_general(grad, w_out[...], (((1,), (1,)), ((), ())), preferred_element_type=f32)
    slopes = cdf + preact * jnp.exp(-0.5 * preact * preact) * 0.3989422804014327
    d_pre = (d_hidden * slopes).astype(bf16)
    contract = (((0,), (0,)), ((), ()))
    acc_out[...] += lax.dot_general(grad, hidden, contract, preferred_element_type=f32)
    acc_in[...] += lax.dot_general(normed, d_pre, contract, preferred_element_type=f32)
    d_norm = lax.dot_general(d_pre, w_in[...], (((1,), (1,)), ((), ())), preferred_element_type=f32)
    scaled = d_norm * gain[...]
    dz = inverse * (
        scaled
        - jnp.mean(scaled, axis=-1, keepdims=True)
        - unit * jnp.mean(scaled * unit, axis=-1, keepdims=True)
    )
    write_cells(dz_out, first, step, segs, dz)
    own = read_cells(masked, first, step, segs)
    keep = read_cells(ocean, first, step, segs)
    write_cells(advanced, first, step, segs, own + keep * out)
    grads = dz.astype(bf16).astype(f32)
    per_row = sum(w for _, w in segs)
    for tap in range(7):
        for col in range(7):
            total = None
            for row in range(step):
                at = row * per_row
                for pad, start, width in pads:
                    cells = pad[first + row + tap, start + col : start + col + width, :]
                    product = cells * grads[at : at + width]
                    at += width
                    for part in range(0, width, 8):
                        piece = product[part : part + 8]
                        total = piece if total is None else total + piece
            acc_tap[tap * 7 + col] += total


def inside_kernel(
    flags, masked, lat_a, lat_b, gmask, ocean, taps, gain, w_in, b_in, w_out,
    advanced, dz_out, acc_in, acc_out, acc_tap, pad,
):
    fill_rows(pad, masked, flags, lat_a, lat_b, 0, COLS, 0)
    for acc in (acc_in, acc_out, acc_tap):
        acc[...] = jnp.zeros_like(acc)
    params = (taps, gain, w_in, b_in, w_out)

    def block(index, carry):
        main_rows(16, INSIDE, ((pad, 5, 32),), masked, gmask, ocean, params, advanced, dz_out, (acc_in, acc_out, acc_tap), index)
        return carry

    lax.fori_loop(0, ROWS // 16, block, 0)


def strips_kernel(
    flags, masked, lat_a, lat_b, lon_a, lon_b, gmask, ocean, taps, gain, w_in, b_in, w_out,
    had_advanced, had_dz, had_in, had_out, had_tap,
    advanced, dz_out, terms, left, right, acc_in, acc_out, acc_tap, lines,
):
    fill_strips(left, right, masked, flags, lat_a, lat_b, lon_a, lon_b)
    advanced[:, 8:40, :] = had_advanced[:, 8:40, :]
    dz_out[:, 8:40, :] = had_dz[:, 8:40, :]
    acc_in[...] = had_in[...]
    acc_out[...] = had_out[...]
    acc_tap[...] = had_tap[...]
    params = (taps, gain, w_in, b_in, w_out)

    def block(index, carry):
        main_rows(32, STRIPS, ((left, 5, 8), (right, 5, 8)), masked, gmask, ocean, params, advanced, dz_out, (acc_in, acc_out, acc_tap), index)
        return carry

    lax.fori_loop(0, ROWS // 32, block, 0)
    lines[0:C, :] = acc_in[:, 0:C]
    lines[C : 2 * C, :] = acc_in[:, C:]
    lines[2 * C : 2 * C + FF, :] = acc_out[...].T
    lines[512:561, :] = jnp.sum(acc_tap[...], axis=1)
    lines[561:576, :] = jnp.zeros((15, C), jnp.float32)
    chunk = terms.shape[1]
    for part in range(terms.shape[0]):
        terms[part] = lines[part * chunk : (part + 1) * chunk, :].astype(LINK)


def back_kernel(flags, dz, lon_a, lon_b, lat_a, lat_b, gmask, ocean, taps, field_grad, pad):
    f32 = jnp.float32
    even = flags[1] == 0
    from_a, from_b = lon_a[...].astype(f32), lon_b[...].astype(f32)
    pad[3 : 3 + ROWS, 8 : 8 + COLS, :] = dz[...].astype(f32)
    pad[3 : 3 + ROWS, 5:8, :] = jnp.where(even, from_b, from_a)
    pad[3 : 3 + ROWS, 8 + COLS : 11 + COLS, :] = jnp.where(even, from_a, from_b)
    even = flags[0] == 0
    from_a, from_b = lat_a[...].astype(f32), lat_b[...].astype(f32)
    pad[0:3, 5 : 11 + COLS, :] = jnp.where(even, from_b, from_a)
    pad[3 + ROWS : 6 + ROWS, 5 : 11 + COLS, :] = jnp.where(even, from_a, from_b)

    def block(index, carry):
        back_rows(4, ((0, COLS),), ((pad, 5, COLS),), gmask, ocean, taps, field_grad, index)
        return carry

    lax.fori_loop(0, ROWS // 4, block, 0)


def back_rows(step, segs, pads, gmask, ocean, taps, field_grad, index):
    first = index * step
    back = conv_rows(pads, taps, first, step, True)
    own = read_cells(gmask, first, step, segs)
    keep = read_cells(ocean, first, step, segs)
    write_cells(field_grad, first, step, segs, own + keep * back)


def final_kernel(parts, kernel_grad, w_in_grad, w_out_grad, lines, *, factor):
    chunk = parts.shape[1]
    for part in range(parts.shape[0]):
        lines[part * chunk : (part + 1) * chunk, :] = parts[part].astype(jnp.float32) * factor
    w_in_grad[:, 0:C] = lines[0:C, :]
    w_in_grad[:, C:] = lines[C : 2 * C, :]
    w_out_grad[...] = lines[2 * C : 2 * C + FF, :]
    kernel_grad[...] = lines[512:561, :]


def call(body, args, outs, scratch, flops):
    vmem = pl.BlockSpec(memory_space=pltpu.VMEM)
    smem = pl.BlockSpec(memory_space=pltpu.SMEM)
    return pl.pallas_call(
        body,
        out_shape=outs,
        in_specs=[smem if a.dtype == jnp.int32 else vmem for a in args],
        out_specs=[vmem] * len(outs),
        scratch_shapes=scratch,
        compiler_params=pltpu.CompilerParams(vmem_limit_bytes=40 << 20),
        cost_estimate=pl.CostEstimate(flops=flops, bytes_accessed=2 << 20, transcendentals=1 << 19),
    )(*args)


def kind(*shape, dtype=jnp.float32):
    return jax.ShapeDtypeStruct(shape, dtype)


CELLS = kind(ROWS, COLS, C, dtype=jnp.bfloat16)
WIDE = pltpu.VMEM((ROWS + 6, COLS, C), jnp.float32)
PADDED = pltpu.VMEM((ROWS + 6, COLS + 16, C), jnp.float32)
NARROW = pltpu.VMEM((ROWS + 6, 24, C), jnp.float32)
SUMS = ((C, FF), (C, FF), (49, 8, C))


def group_size(axes):
    size = 1
    for axis in axes:
        size *= lax.axis_size(axis)
    return size


def exchange(low, high, axes, count, wraps):
    even = lax.axis_index(axes[-1]) % 2 == 0
    joins = [i for i in range(1, count, 2) if wraps or i + 1 < count]
    pairs_b = [(i, (i + 1) % count) for i in joins] + [((i + 1) % count, i) for i in joins]
    pairs_a = [(i, i + 1) for i in range(0, count, 2)] + [(i + 1, i) for i in range(0, count, 2)]
    from_b = lax.ppermute(jnp.where(even, low, high), axes, pairs_b)
    from_a = lax.ppermute(jnp.where(even, high, low), axes, pairs_a)
    return from_a, from_b


def lat_halo(top, bottom):
    return exchange(top, bottom, LAT, group_size(LAT), False)


def lon_halo(head, tail, lat_a, lat_b):
    even = lax.axis_index(LAT[-1]) % 2 == 0
    north = jnp.where(even, lat_b, lat_a)
    south = jnp.where(even, lat_a, lat_b)
    head = jnp.concatenate([north[:, :3], head, south[:, :3]])
    tail = jnp.concatenate([north[:, COLS - 3 :], tail, south[:, COLS - 3 :]])
    return exchange(head, tail, LON, group_size(LON), True)


def grid_sum(parts):
    size, chunk, _ = parts.shape
    parts = lax.all_to_all(parts, OUTER, 0, 0, tiled=True)
    own = jnp.sum(parts.astype(jnp.float32), axis=0)
    count = group_size(INNER)
    copies = jnp.broadcast_to(own[None], (count, chunk, C))
    total = jnp.sum(lax.all_to_all(copies, INNER, 0, 0, tiled=True), axis=0)
    spread = jnp.broadcast_to(total.astype(LINK)[None], (size, chunk, C))
    return lax.all_to_all(spread, OUTER, 0, 0, tiled=True)


def shards(fields, ocean, cotangent, kernel, ln_gain, w_in, b_in, w_out):
    flags = jnp.stack([lax.axis_index(LAT[-1]) % 2, lax.axis_index(LON[-1]) % 2]).astype(jnp.int32)
    taps = kernel.reshape(49, C)
    params = (taps, ln_gain.reshape(1, C), w_in, b_in.reshape(1, FF), w_out)

    def edge(rows, cols):
        return fields[rows, cols] * ocean[rows, cols].astype(jnp.bfloat16)[..., None]

    every = slice(None)
    top, bottom = edge(slice(0, 3), every), edge(slice(ROWS - 3, ROWS), every)
    head, tail = edge(every, slice(0, 3)), edge(every, slice(COLS - 3, COLS))
    lat = lat_halo(top, bottom)
    lon = lon_halo(head, tail, *lat)
    ocean_b = jnp.broadcast_to(ocean.astype(jnp.bfloat16)[..., None], fields.shape)
    masked = fields * ocean_b
    gmask = cotangent * ocean_b
    scratch = [pltpu.VMEM(shape, jnp.float32) for shape in SUMS]
    inside = call(
        inside_kernel,
        (flags, masked, *lat, gmask, ocean_b, *params),
        [CELLS, CELLS, *(kind(*shape) for shape in SUMS)],
        [WIDE],
        350_000_000,
    )
    parts = group_size(OUTER)
    advanced, dz, terms = call(
        strips_kernel,
        (flags, masked, *lat, *lon, gmask, ocean_b, *params, *inside),
        [CELLS, CELLS, kind(parts, TERM_ROWS // parts, C, dtype=LINK)],
        [NARROW, NARROW, *scratch, pltpu.VMEM((TERM_ROWS, C), jnp.float32)],
        170_000_000,
    )
    sums = grid_sum(terms)
    lon_a, lon_b = exchange(dz[:, :3], dz[:, COLS - 3 :], LON, group_size(LON), True)
    even = flags[1] == 0
    west, east = jnp.where(even, lon_b, lon_a), jnp.where(even, lon_a, lon_b)

    def full(rows):
        return jnp.concatenate([west[rows], dz[rows], east[rows]], axis=1)

    lat = exchange(full(slice(0, 3)), full(slice(ROWS - 3, ROWS)), LAT, group_size(LAT), False)
    (field_grad,) = call(
        back_kernel, (flags, dz, lon_a, lon_b, *lat, gmask, ocean_b, taps), [CELLS], [PADDED], 100_000_000
    )
    cells = ROWS * COLS * group_size(LAT) * group_size(LON)
    kernel_grad, w_in_grad, w_out_grad = call(
        functools.partial(final_kernel, factor=cells**-0.5),
        (sums,),
        [kind(49, C), kind(C, FF), kind(FF, C)],
        [pltpu.VMEM((TERM_ROWS, C), jnp.float32)],
        1_000_000,
    )
    return (advanced, field_grad, kernel_grad.reshape(7, 7, C), w_in_grad, w_out_grad)


def solution(mesh):
    torus = Mesh(mesh.devices.reshape(4, 2, 12, 4, 2), LON + LAT)
    cells = P(LAT, LON, None)
    in_specs = (cells, P(LAT, LON), cells, P(), P(), P(), P(), P())
    out_specs = (cells, cells, P(), P(), P())
    return jax.shard_map(shards, mesh=torus, in_specs=in_specs, out_specs=out_specs, check_vma=False)
```

```python
import functools

import jax
import jax.numpy as jnp
from jax import lax
from jax.experimental import pallas as pl
from jax.experimental.pallas import tpu as pltpu
from jax.sharding import Mesh
from jax.sharding import PartitionSpec as P

LINK = jnp.bfloat16
LON = ("x", "yh", "z")
LAT = ("yl", "core")
OUTER = ("x", "yh", "yl", "core")
INNER = ("z",)
ROWS = 32
COLS = 48
C = 128
FF = 256
TERM_ROWS = 576


INSIDE = ((8, 32),)
STRIPS = ((0, 8), (40, 8))


def fill_rows(pad, own, flags, halo_a, halo_b, first, last, at):
    f32 = jnp.float32
    even = flags[0] == 0
    pad[3 : 3 + ROWS, at : at + last - first, :] = own[:, first:last, :].astype(f32)
    from_a = halo_a[:, first:last, :].astype(f32)
    from_b = halo_b[:, first:last, :].astype(f32)
    pad[0:3, at : at + last - first, :] = jnp.where(even, from_b, from_a)
    pad[3 + ROWS : 6 + ROWS, at : at + last - first, :] = jnp.where(even, from_a, from_b)


def fill_strips(left, right, own, flags, lat_a, lat_b, lon_a, lon_b):
    f32 = jnp.float32
    even = flags[1] == 0
    fill_rows(left, own, flags, lat_a, lat_b, 0, 16, 8)
    fill_rows(right, own, flags, lat_a, lat_b, 32, 48, 0)
    from_a, from_b = lon_a[...].astype(f32), lon_b[...].astype(f32)
    left[:, 5:8, :] = jnp.where(even, from_b, from_a)
    right[:, 16:19, :] = jnp.where(even, from_a, from_b)


def conv_rows(pads, taps, first, step, flip):
    sums = [[jnp.zeros((width, C), jnp.float32) for _, _, width in pads] for _ in range(step)]
    for row in range(step + 6):
        for col in range(7):
            for seg, (pad, start, width) in enumerate(pads):
                cells = pad[first + row, start + col : start + col + width, :]
                for out in range(step):
                    tap = row - out
                    if 0 <= tap < 7:
                        at = tap * 7 + col
                        at = 48 - at if flip else at
                        sums[out][seg] = sums[out][seg] + cells * taps[at : at + 1, :]
    return jnp.concatenate([part for line in sums for part in line], axis=0)


def read_cells(ref, first, step, segs):
    return jnp.concatenate(
        [ref[first + row, c : c + w, :].astype(jnp.float32) for row in range(step) for c, w in segs], axis=0
    )


def write_cells(ref, first, step, segs, values):
    at = 0
    for row in range(step):
        for c, w in segs:
            ref[first + row, c : c + w, :] = values[at : at + w].astype(jnp.bfloat16)
            at += w


def main_rows(step, segs, pads, masked, gmask, ocean, params, advanced, dz_out, sums, index):
    f32, bf16 = jnp.float32, jnp.bfloat16
    taps, gain, w_in, b_in, w_out = params
    acc_in, acc_out, acc_tap = sums
    first = index * step
    z = conv_rows(pads, taps, first, step, False)
    grad = read_cells(gmask, first, step, segs).astype(bf16)
    average = jnp.mean(z, axis=-1, keepdims=True)
    centre = z - average
    inverse = lax.rsqrt(jnp.mean(centre * centre, axis=-1, keepdims=True) + 1e-06)
    unit = centre * inverse
    normed = (unit * gain[...]).astype(bf16)
    preact = jnp.dot(normed, w_in[...], preferred_element_type=f32) + b_in[...]
    cdf = 0.5 * (1.0 + lax.erf(preact * 0.7071067811865476))
    hidden = (preact * cdf).astype(bf16)
    out = jnp.dot(hidden, w_out[...], preferred_element_type=f32)
    d_hidden = lax.dot_general(grad, w_out[...], (((1,), (1,)), ((), ())), preferred_element_type=f32)
    slopes = cdf + preact * jnp.exp(-0.5 * preact * preact) * 0.3989422804014327
    d_pre = (d_hidden * slopes).astype(bf16)
    contract = (((0,), (0,)), ((), ()))
    acc_out[...] += lax.dot_general(grad, hidden, contract, preferred_element_type=f32)
    acc_in[...] += lax.dot_general(normed, d_pre, contract, preferred_element_type=f32)
    d_norm = lax.dot_general(d_pre, w_in[...], (((1,), (1,)), ((), ())), preferred_element_type=f32)
    scaled = d_norm * gain[...]
    dz = inverse * (
        scaled
        - jnp.mean(scaled, axis=-1, keepdims=True)
        - unit * jnp.mean(scaled * unit, axis=-1, keepdims=True)
    )
    write_cells(dz_out, first, step, segs, dz)
    own = read_cells(masked, first, step, segs)
    keep = read_cells(ocean, first, step, segs)
    write_cells(advanced, first, step, segs, own + keep * out)
    grads = dz.astype(bf16).astype(f32)
    per_row = sum(w for _, w in segs)
    for tap in range(7):
        for col in range(7):
            total = None
            for row in range(step):
                at = row * per_row
                for pad, start, width in pads:
                    cells = pad[first + row + tap, start + col : start + col + width, :]
                    product = cells * grads[at : at + width]
                    at += width
                    for part in range(0, width, 8):
                        piece = product[part : part + 8]
                        total = piece if total is None else total + piece
            acc_tap[tap * 7 + col] += total


def inside_kernel(
    flags, masked, lat_a, lat_b, gmask, ocean, taps, gain, w_in, b_in, w_out,
    advanced, dz_out, acc_in, acc_out, acc_tap, pad,
):
    fill_rows(pad, masked, flags, lat_a, lat_b, 0, COLS, 0)
    for acc in (acc_in, acc_out, acc_tap):
        acc[...] = jnp.zeros_like(acc)
    params = (taps, gain, w_in, b_in, w_out)

    def block(index, carry):
        main_rows(16, INSIDE, ((pad, 5, 32),), masked, gmask, ocean, params, advanced, dz_out, (acc_in, acc_out, acc_tap), index)
        return carry

    lax.fori_loop(0, ROWS // 16, block, 0)


def strips_kernel(
    flags, masked, lat_a, lat_b, lon_a, lon_b, gmask, ocean, taps, gain, w_in, b_in, w_out,
    had_advanced, had_dz, had_in, had_out, had_tap,
    advanced, dz_out, terms, left, right, acc_in, acc_out, acc_tap, lines,
):
    fill_strips(left, right, masked, flags, lat_a, lat_b, lon_a, lon_b)
    advanced[:, 8:40, :] = had_advanced[:, 8:40, :]
    dz_out[:, 8:40, :] = had_dz[:, 8:40, :]
    acc_in[...] = had_in[...]
    acc_out[...] = had_out[...]
    acc_tap[...] = had_tap[...]
    params = (taps, gain, w_in, b_in, w_out)

    def block(index, carry):
        main_rows(32, STRIPS, ((left, 5, 8), (right, 5, 8)), masked, gmask, ocean, params, advanced, dz_out, (acc_in, acc_out, acc_tap), index)
        return carry

    lax.fori_loop(0, ROWS // 32, block, 0)
    lines[0:C, :] = acc_in[:, 0:C]
    lines[C : 2 * C, :] = acc_in[:, C:]
    lines[2 * C : 2 * C + FF, :] = acc_out[...].T
    lines[512:561, :] = jnp.sum(acc_tap[...], axis=1)
    lines[561:576, :] = jnp.zeros((15, C), jnp.float32)
    chunk = terms.shape[1]
    for part in range(terms.shape[0]):
        terms[part] = lines[part * chunk : (part + 1) * chunk, :].astype(LINK)


def back_kernel(flags, dz, lon_a, lon_b, lat_a, lat_b, gmask, ocean, taps, field_grad, pad):
    f32 = jnp.float32
    even = flags[1] == 0
    from_a, from_b = lon_a[...].astype(f32), lon_b[...].astype(f32)
    pad[3 : 3 + ROWS, 8 : 8 + COLS, :] = dz[...].astype(f32)
    pad[3 : 3 + ROWS, 5:8, :] = jnp.where(even, from_b, from_a)
    pad[3 : 3 + ROWS, 8 + COLS : 11 + COLS, :] = jnp.where(even, from_a, from_b)
    even = flags[0] == 0
    from_a, from_b = lat_a[...].astype(f32), lat_b[...].astype(f32)
    pad[0:3, 5 : 11 + COLS, :] = jnp.where(even, from_b, from_a)
    pad[3 + ROWS : 6 + ROWS, 5 : 11 + COLS, :] = jnp.where(even, from_a, from_b)

    def block(index, carry):
        back_rows(4, ((0, COLS),), ((pad, 5, COLS),), gmask, ocean, taps, field_grad, index)
        return carry

    lax.fori_loop(0, ROWS // 4, block, 0)


def back_rows(step, segs, pads, gmask, ocean, taps, field_grad, index):
    first = index * step
    back = conv_rows(pads, taps, first, step, True)
    own = read_cells(gmask, first, step, segs)
    keep = read_cells(ocean, first, step, segs)
    write_cells(field_grad, first, step, segs, own + keep * back)


def final_kernel(parts, kernel_grad, w_in_grad, w_out_grad, lines, *, factor):
    chunk = parts.shape[1]
    for part in range(parts.shape[0]):
        lines[part * chunk : (part + 1) * chunk, :] = parts[part].astype(jnp.float32) * factor
    w_in_grad[:, 0:C] = lines[0:C, :]
    w_in_grad[:, C:] = lines[C : 2 * C, :]
    w_out_grad[...] = lines[2 * C : 2 * C + FF, :]
    for row in range(7):
        kernel_grad[row] = lines[512 + 7 * row : 519 + 7 * row, :]


def call(body, args, outs, scratch, flops):
    vmem = pl.BlockSpec(memory_space=pltpu.VMEM)
    smem = pl.BlockSpec(memory_space=pltpu.SMEM)
    return pl.pallas_call(
        body,
        out_shape=outs,
        in_specs=[smem if a.dtype == jnp.int32 else vmem for a in args],
        out_specs=[vmem] * len(outs),
        scratch_shapes=scratch,
        compiler_params=pltpu.CompilerParams(vmem_limit_bytes=40 << 20),
        cost_estimate=pl.CostEstimate(flops=flops, bytes_accessed=2 << 20, transcendentals=1 << 19),
    )(*args)


def kind(*shape, dtype=jnp.float32):
    return jax.ShapeDtypeStruct(shape, dtype)


CELLS = kind(ROWS, COLS, C, dtype=jnp.bfloat16)
WIDE = pltpu.VMEM((ROWS + 6, COLS, C), jnp.float32)
PADDED = pltpu.VMEM((ROWS + 6, COLS + 16, C), jnp.float32)
NARROW = pltpu.VMEM((ROWS + 6, 24, C), jnp.float32)
SUMS = ((C, FF), (C, FF), (49, 8, C))


def group_size(axes):
    size = 1
    for axis in axes:
        size *= lax.axis_size(axis)
    return size


def swap(values, axes, count, first, wraps):
    starts = [i for i in range(first, count, 2) if wraps or i + 1 < count]
    pairs = [(i, (i + 1) % count) for i in starts] + [((i + 1) % count, i) for i in starts]
    return lax.ppermute(values, axes, pairs)


def exchange(low, high, axes, count, wraps):
    even = lax.axis_index(axes[-1]) % 2 == 0
    from_b = swap(jnp.where(even, low, high), axes, count, 1, wraps)
    from_a = swap(jnp.where(even, high, low), axes, count, 0, wraps)
    return from_a, from_b


def lat_halo(top, bottom):
    return exchange(top, bottom, LAT, group_size(LAT), False)


def lon_halo(head, tail, lat_a, lat_b):
    even = lax.axis_index(LAT[-1]) % 2 == 0
    north = jnp.where(even, lat_b, lat_a)
    south = jnp.where(even, lat_a, lat_b)
    head = jnp.concatenate([north[:, :3], head, south[:, :3]])
    tail = jnp.concatenate([north[:, COLS - 3 :], tail, south[:, COLS - 3 :]])
    return exchange(head, tail, LON, group_size(LON), True)


def scatter_sum(parts):
    return jnp.sum(lax.all_to_all(parts, OUTER, 0, 0, tiled=True).astype(jnp.float32), axis=0)


def inner_sum(own):
    copies = jnp.broadcast_to(own[None], (group_size(INNER), *own.shape))
    return jnp.sum(lax.all_to_all(copies, INNER, 0, 0, tiled=True), axis=0).astype(LINK)


def hand_out(total):
    spread = jnp.broadcast_to(total[None], (group_size(OUTER), *total.shape))
    return lax.all_to_all(spread, OUTER, 0, 0, tiled=True)


def shards(fields, ocean, cotangent, kernel, ln_gain, w_in, b_in, w_out):
    flags = jnp.stack([lax.axis_index(LAT[-1]) % 2, lax.axis_index(LON[-1]) % 2]).astype(jnp.int32)
    taps = kernel.reshape(49, C)
    params = (taps, ln_gain.reshape(1, C), w_in, b_in.reshape(1, FF), w_out)

    def edge(rows, cols):
        return fields[rows, cols] * ocean[rows, cols].astype(jnp.bfloat16)[..., None]

    every = slice(None)
    lat = lat_halo(edge(slice(0, 3), every), edge(slice(ROWS - 3, ROWS), every))
    ocean_b = jnp.broadcast_to(ocean.astype(jnp.bfloat16)[..., None], fields.shape)
    masked = fields * ocean_b
    gmask = cotangent * ocean_b
    lon = lon_halo(masked[:, :3], masked[:, COLS - 3 :], *lat)
    scratch = [pltpu.VMEM(shape, jnp.float32) for shape in SUMS]
    inside = call(
        inside_kernel,
        (flags, masked, *lat, gmask, ocean_b, *params),
        [CELLS, CELLS, *(kind(*shape) for shape in SUMS)],
        [WIDE],
        350_000_000,
    )
    parts = group_size(OUTER)
    advanced, dz, terms = call(
        strips_kernel,
        (flags, masked, *lat, *lon, gmask, ocean_b, *params, *inside),
        [CELLS, CELLS, kind(parts, TERM_ROWS // parts, C, dtype=LINK)],
        [NARROW, NARROW, *scratch, pltpu.VMEM((TERM_ROWS, C), jnp.float32)],
        170_000_000,
    )
    own = scatter_sum(terms)
    even = flags[1] == 0
    low, high = dz[:, :3], dz[:, COLS - 3 :]
    lon_b = swap(jnp.where(even, low, high), LON, group_size(LON), 1, True)
    near, own = lax.optimization_barrier((jnp.where(even, high, low), own))
    lon_a = swap(near, LON, group_size(LON), 0, True)
    west, east = jnp.where(even, lon_b, lon_a), jnp.where(even, lon_a, lon_b)

    def full(rows):
        return jnp.concatenate([west[rows], dz[rows], east[rows]], axis=1)

    lat = exchange(full(slice(0, 3)), full(slice(ROWS - 3, ROWS)), LAT, group_size(LAT), False)
    total, *lat = lax.optimization_barrier((inner_sum(own), *lat))
    sums = hand_out(total)
    (field_grad,) = call(
        back_kernel, (flags, dz, lon_a, lon_b, *lat, gmask, ocean_b, taps), [CELLS], [PADDED], 100_000_000
    )
    cells = ROWS * COLS * group_size(LAT) * group_size(LON)
    kernel_grad, w_in_grad, w_out_grad = call(
        functools.partial(final_kernel, factor=cells**-0.5),
        (sums,),
        [kind(7, 7, C), kind(C, FF), kind(FF, C)],
        [pltpu.VMEM((TERM_ROWS, C), jnp.float32)],
        1_000_000,
    )
    return (advanced, field_grad, kernel_grad, w_in_grad, w_out_grad)


def solution(mesh):
    torus = Mesh(mesh.devices.reshape(4, 2, 12, 4, 2), LON + LAT)
    cells = P(LAT, LON, None)
    in_specs = (cells, P(LAT, LON), cells, P(), P(), P(), P(), P())
    out_specs = (cells, cells, P(), P(), P())
    return jax.shard_map(shards, mesh=torus, in_specs=in_specs, out_specs=out_specs, check_vma=False)
```

```python
import functools

import jax
import jax.numpy as jnp
from jax import lax
from jax.experimental import pallas as pl
from jax.experimental.pallas import tpu as pltpu
from jax.sharding import Mesh
from jax.sharding import PartitionSpec as P

LINK = jnp.bfloat16
LON = ("x", "yh", "z")
LAT = ("yl", "core")
OUTER = ("x", "yh", "yl", "core")
INNER = ("z",)
ROWS = 32
COLS = 48
C = 128
FF = 256
TERM_ROWS = 576


INSIDE = ((8, 32),)
STRIPS = ((0, 8), (40, 8))
INSIDE_OUT = ((0, 32),)
STRIPS_OUT = ((0, 8), (8, 8))


def fill_rows(pad, own, flags, halo_a, halo_b, first, last, at):
    f32 = jnp.float32
    even = flags[0] == 0
    pad[3 : 3 + ROWS, at : at + last - first, :] = own[:, first:last, :].astype(f32)
    from_a = halo_a[:, first:last, :].astype(f32)
    from_b = halo_b[:, first:last, :].astype(f32)
    pad[0:3, at : at + last - first, :] = jnp.where(even, from_b, from_a)
    pad[3 + ROWS : 6 + ROWS, at : at + last - first, :] = jnp.where(even, from_a, from_b)


def fill_strips(left, right, own, flags, lat_a, lat_b, lon_a, lon_b):
    f32 = jnp.float32
    even = flags[1] == 0
    fill_rows(left, own, flags, lat_a, lat_b, 0, 16, 8)
    fill_rows(right, own, flags, lat_a, lat_b, 32, 48, 0)
    from_a, from_b = lon_a[...].astype(f32), lon_b[...].astype(f32)
    left[:, 5:8, :] = jnp.where(even, from_b, from_a)
    right[:, 16:19, :] = jnp.where(even, from_a, from_b)


def conv_rows(pads, taps, first, step, flip):
    sums = [[jnp.zeros((width, C), jnp.float32) for _, _, width in pads] for _ in range(step)]
    for row in range(step + 6):
        for col in range(7):
            for seg, (pad, start, width) in enumerate(pads):
                cells = pad[first + row, start + col : start + col + width, :]
                for out in range(step):
                    tap = row - out
                    if 0 <= tap < 7:
                        at = tap * 7 + col
                        at = 48 - at if flip else at
                        sums[out][seg] = sums[out][seg] + cells * taps[at : at + 1, :]
    return jnp.concatenate([part for line in sums for part in line], axis=0)


def read_cells(ref, first, step, segs):
    return jnp.concatenate(
        [ref[first + row, c : c + w, :].astype(jnp.float32) for row in range(step) for c, w in segs], axis=0
    )


def write_cells(ref, first, step, segs, values):
    at = 0
    for row in range(step):
        for c, w in segs:
            ref[first + row, c : c + w, :] = values[at : at + w].astype(jnp.bfloat16)
            at += w


def main_rows(step, segs, outs, pads, gmask, params, hidden_out, dz_out, sums, index):
    f32, bf16 = jnp.float32, jnp.bfloat16
    taps, gain, w_in, b_in, w_out = params
    acc_in, acc_out, acc_tap = sums
    first = index * step
    z = conv_rows(pads, taps, first, step, False)
    grad = read_cells(gmask, first, step, segs).astype(bf16)
    average = jnp.mean(z, axis=-1, keepdims=True)
    centre = z - average
    inverse = lax.rsqrt(jnp.mean(centre * centre, axis=-1, keepdims=True) + 1e-06)
    unit = centre * inverse
    normed = (unit * gain[...]).astype(bf16)
    preact = jnp.dot(normed, w_in[...], preferred_element_type=f32) + b_in[...]
    cdf = 0.5 * (1.0 + lax.erf(preact * 0.7071067811865476))
    hidden = (preact * cdf).astype(bf16)
    hidden_out[pl.ds(index * hidden.shape[0], hidden.shape[0]), :] = hidden
    d_hidden = lax.dot_general(grad, w_out[...], (((1,), (1,)), ((), ())), preferred_element_type=f32)
    slopes = cdf + preact * jnp.exp(-0.5 * preact * preact) * 0.3989422804014327
    d_pre = (d_hidden * slopes).astype(bf16)
    contract = (((0,), (0,)), ((), ()))
    acc_out[...] += lax.dot_general(grad, hidden, contract, preferred_element_type=f32)
    acc_in[...] += lax.dot_general(normed, d_pre, contract, preferred_element_type=f32)
    d_norm = lax.dot_general(d_pre, w_in[...], (((1,), (1,)), ((), ())), preferred_element_type=f32)
    scaled = d_norm * gain[...]
    dz = inverse * (
        scaled
        - jnp.mean(scaled, axis=-1, keepdims=True)
        - unit * jnp.mean(scaled * unit, axis=-1, keepdims=True)
    )
    write_cells(dz_out, first, step, outs, dz)
    grads = dz.astype(bf16).astype(f32)
    per_row = sum(w for _, w in segs)
    for tap in range(7):
        for col in range(7):
            total = None
            for row in range(step):
                at = row * per_row
                for pad, start, width in pads:
                    cells = pad[first + row + tap, start + col : start + col + width, :]
                    product = cells * grads[at : at + width]
                    at += width
                    for part in range(0, width, 8):
                        piece = product[part : part + 8]
                        total = piece if total is None else total + piece
            acc_tap[tap * 7 + col] += total


def inside_kernel(
    flags, masked, lat_b, lat_a, gmask, taps, gain, w_in, b_in, w_out,
    hidden, dz_out, acc_in, acc_out, acc_tap, pad,
):
    fill_rows(pad, masked, flags, lat_a, lat_b, 0, COLS, 0)
    for acc in (acc_in, acc_out, acc_tap):
        acc[...] = jnp.zeros_like(acc)
    params = (taps, gain, w_in, b_in, w_out)
    sums = (acc_in, acc_out, acc_tap)

    def block(index, carry):
        main_rows(16, INSIDE, INSIDE_OUT, ((pad, 5, 32),), gmask, params, hidden, dz_out, sums, index)
        return carry

    lax.fori_loop(0, ROWS // 16, block, 0)


def strips_kernel(
    flags, masked, lat_b, lat_a, lon_b, lon_a, gmask, taps, gain, w_in, b_in, w_out,
    had_in, had_out, had_tap,
    hidden, dz_out, terms, left, right, acc_in, acc_out, acc_tap,
):
    fill_strips(left, right, masked, flags, lat_a, lat_b, lon_a, lon_b)
    acc_in[...] = had_in[...]
    acc_out[...] = had_out[...]
    acc_tap[...] = had_tap[...]
    params = (taps, gain, w_in, b_in, w_out)
    pads = ((left, 5, 8), (right, 5, 8))
    main_rows(ROWS, STRIPS, STRIPS_OUT, pads, gmask, params, hidden, dz_out, (acc_in, acc_out, acc_tap), 0)
    half = C // 8
    turned = acc_out[...].T
    tap_sums = jnp.sum(acc_tap[...], axis=1)
    for part in range(half):
        rows = slice(8 * part, 8 * part + 8)
        terms[part, 0:8, :] = acc_in[rows, 0:C].astype(LINK)
        terms[half + part, 0:8, :] = acc_in[rows, C:].astype(LINK)
    for part in range(2 * half):
        terms[2 * half + part, 0:8, :] = turned[8 * part : 8 * part + 8].astype(LINK)
    for part in range(terms.shape[0]):
        row = tap_sums[part : part + 1] if part < 49 else jnp.zeros((1, C), jnp.float32)
        terms[part, 8:9, :] = row.astype(LINK)


def advance_kernel(hidden_in, hidden_st, masked, ocean, w_out, advanced):
    f32 = jnp.float32

    def block(index, carry):
        first = index * 8
        for hidden, segs, outs in ((hidden_in, INSIDE, INSIDE_OUT), (hidden_st, STRIPS, STRIPS_OUT)):
            width = sum(w for _, w in outs)
            size = 8 * width
            out = jnp.dot(hidden[pl.ds(index * size, size), :], w_out[...], preferred_element_type=f32)
            own = read_cells(masked, first, 8, segs)
            keep = read_cells(ocean, first, 8, segs)
            write_cells(advanced, first, 8, segs, own + keep * out)
        return carry

    lax.fori_loop(0, ROWS // 8, block, 0)


def back_kernel(flags, dz_in, dz_st, lon_b, lon_a, lat_b, lat_a, gmask, ocean, taps, field_grad, pad):
    f32 = jnp.float32
    even = flags[1] == 0
    from_a, from_b = lon_a[...].astype(f32), lon_b[...].astype(f32)
    pad[3 : 3 + ROWS, 8:16, :] = dz_st[:, 0:8, :].astype(f32)
    pad[3 : 3 + ROWS, 16:48, :] = dz_in[...].astype(f32)
    pad[3 : 3 + ROWS, 48:56, :] = dz_st[:, 8:16, :].astype(f32)
    pad[3 : 3 + ROWS, 5:8, :] = jnp.where(even, from_b, from_a)
    pad[3 : 3 + ROWS, 8 + COLS : 11 + COLS, :] = jnp.where(even, from_a, from_b)
    even = flags[0] == 0
    from_a, from_b = lat_a[...].astype(f32), lat_b[...].astype(f32)
    pad[0:3, 5 : 11 + COLS, :] = jnp.where(even, from_b, from_a)
    pad[3 + ROWS : 6 + ROWS, 5 : 11 + COLS, :] = jnp.where(even, from_a, from_b)

    def block(index, carry):
        back_rows(4, ((0, COLS),), ((pad, 5, COLS),), gmask, ocean, taps, field_grad, index)
        return carry

    lax.fori_loop(0, ROWS // 4, block, 0)


def back_rows(step, segs, pads, gmask, ocean, taps, field_grad, index):
    first = index * step
    back = conv_rows(pads, taps, first, step, True)
    own = read_cells(gmask, first, step, segs)
    keep = read_cells(ocean, first, step, segs)
    write_cells(field_grad, first, step, segs, own + keep * back)


def final_kernel(parts, kernel_grad, w_in_grad, w_out_grad, *, factor):
    half = C // 8
    for part in range(parts.shape[0]):
        rows = parts[part, 0:8, :].astype(jnp.float32) * factor
        if part < half:
            w_in_grad[8 * part : 8 * part + 8, 0:C] = rows
        elif part < 2 * half:
            w_in_grad[8 * (part - half) : 8 * (part - half) + 8, C:] = rows
        else:
            w_out_grad[8 * (part - 2 * half) : 8 * (part - 2 * half) + 8, :] = rows
    for part in range(49):
        kernel_grad[part // 7, part % 7 : part % 7 + 1, :] = parts[part, 8:9, :].astype(jnp.float32) * factor


def call(body, args, outs, scratch, flops):
    vmem = pl.BlockSpec(memory_space=pltpu.VMEM)
    smem = pl.BlockSpec(memory_space=pltpu.SMEM)
    return pl.pallas_call(
        body,
        out_shape=outs,
        in_specs=[smem if a.dtype == jnp.int32 else vmem for a in args],
        out_specs=[vmem] * len(outs),
        scratch_shapes=scratch,
        compiler_params=pltpu.CompilerParams(vmem_limit_bytes=40 << 20),
        cost_estimate=pl.CostEstimate(flops=flops, bytes_accessed=2 << 20, transcendentals=1 << 19),
    )(*args)


def kind(*shape, dtype=jnp.float32):
    return jax.ShapeDtypeStruct(shape, dtype)


CELLS = kind(ROWS, COLS, C, dtype=jnp.bfloat16)
WIDE = pltpu.VMEM((ROWS + 6, COLS, C), jnp.float32)
PADDED = pltpu.VMEM((ROWS + 6, COLS + 16, C), jnp.float32)
NARROW = pltpu.VMEM((ROWS + 6, 24, C), jnp.float32)
SUMS = ((C, FF), (C, FF), (49, 8, C))


def group_size(axes):
    size = 1
    for axis in axes:
        size *= lax.axis_size(axis)
    return size


def swap(values, axes, count, first, wraps):
    starts = [i for i in range(first, count, 2) if wraps or i + 1 < count]
    pairs = [(i, (i + 1) % count) for i in starts] + [((i + 1) % count, i) for i in starts]
    return lax.ppermute(values, axes, pairs)


def exchange(low, high, axes, count, wraps):
    even = lax.axis_index(axes[-1]) % 2 == 0
    from_b = swap(jnp.where(even, low, high), axes, count, 1, wraps)
    from_a = swap(jnp.where(even, high, low), axes, count, 0, wraps)
    return from_b, from_a


def lat_halo(top, bottom):
    return exchange(top, bottom, LAT, group_size(LAT), False)


def lon_halo(head, tail, lat_b, lat_a):
    even = lax.axis_index(LAT[-1]) % 2 == 0
    north = jnp.where(even, lat_b, lat_a)
    south = jnp.where(even, lat_a, lat_b)
    head = jnp.concatenate([north[:, :3], head, south[:, :3]])
    tail = jnp.concatenate([north[:, COLS - 3 :], tail, south[:, COLS - 3 :]])
    return exchange(head, tail, LON, group_size(LON), True)


def scatter_sum(parts):
    return jnp.sum(lax.all_to_all(parts, OUTER, 0, 0, tiled=True).astype(jnp.float32), axis=0)


def inner_copies(own):
    return jnp.broadcast_to(own[None], (group_size(INNER), *own.shape))


def inner_sum(copies):
    return jnp.sum(lax.all_to_all(copies, INNER, 0, 0, tiled=True), axis=0).astype(LINK)


def hand_out(total):
    spread = jnp.broadcast_to(total[None], (group_size(OUTER), *total.shape))
    return lax.all_to_all(spread, OUTER, 0, 0, tiled=True)


def shards(fields, ocean, cotangent, kernel, ln_gain, w_in, b_in, w_out):
    flags = jnp.stack([lax.axis_index(LAT[-1]) % 2, lax.axis_index(LON[-1]) % 2]).astype(jnp.int32)
    taps = kernel.reshape(49, C)
    params = (taps, ln_gain.reshape(1, C), w_in, b_in.reshape(1, FF), w_out)

    def edge(rows, cols):
        return fields[rows, cols] * ocean[rows, cols].astype(jnp.bfloat16)[..., None]

    every = slice(None)
    lat = lat_halo(edge(slice(0, 3), every), edge(slice(ROWS - 3, ROWS), every))
    ocean_b = jnp.broadcast_to(ocean.astype(jnp.bfloat16)[..., None], fields.shape)
    masked = fields * ocean_b
    gmask = cotangent * ocean_b
    lon = lon_halo(masked[:, :3], masked[:, COLS - 3 :], *lat)
    scratch = [pltpu.VMEM(shape, jnp.float32) for shape in SUMS]
    hidden_in, dz_in, *sums = call(
        inside_kernel,
        (flags, masked, *lat, gmask, *params),
        [
            kind(ROWS * 32, FF, dtype=jnp.bfloat16),
            kind(ROWS, 32, C, dtype=jnp.bfloat16),
            *(kind(*shape) for shape in SUMS),
        ],
        [WIDE],
        350_000_000,
    )
    parts = group_size(OUTER)
    hidden_st, dz_st, terms = call(
        strips_kernel,
        (flags, masked, *lat, *lon, gmask, *params, *sums),
        [
            kind(ROWS * 16, FF, dtype=jnp.bfloat16),
            kind(ROWS, 16, C, dtype=jnp.bfloat16),
            kind(parts, TERM_ROWS // parts, C, dtype=LINK),
        ],
        [NARROW, NARROW, *scratch],
        170_000_000,
    )
    copies = inner_copies(scatter_sum(terms))
    even = flags[1] == 0
    low, high = dz_st[:, :3], dz_st[:, 13:]
    lon_b = swap(jnp.where(even, low, high), LON, group_size(LON), 1, True)
    (advanced,) = call(
        advance_kernel, (hidden_in, hidden_st, masked, ocean_b, w_out), [CELLS], [], 100_000_000
    )
    near, copies = lax.optimization_barrier((jnp.where(even, high, low), copies))
    lon_a = swap(near, LON, group_size(LON), 0, True)
    west, east = jnp.where(even, lon_b, lon_a), jnp.where(even, lon_a, lon_b)

    def full(rows):
        return jnp.concatenate([west[rows], dz_st[rows, :8], dz_in[rows], dz_st[rows, 8:], east[rows]], axis=1)

    lat = exchange(full(slice(0, 3)), full(slice(ROWS - 3, ROWS)), LAT, group_size(LAT), False)
    sums = hand_out(inner_sum(copies))
    (field_grad,) = call(
        back_kernel, (flags, dz_in, dz_st, lon_b, lon_a, *lat, gmask, ocean_b, taps), [CELLS], [PADDED], 100_000_000
    )
    cells = ROWS * COLS * group_size(LAT) * group_size(LON)
    kernel_grad, w_in_grad, w_out_grad = call(
        functools.partial(final_kernel, factor=cells**-0.5),
        (sums,),
        [kind(7, 7, C), kind(C, FF), kind(FF, C)],
        [],
        1_000_000,
    )
    return (advanced, field_grad, kernel_grad, w_in_grad, w_out_grad)


def solution(mesh):
    torus = Mesh(mesh.devices.reshape(4, 2, 12, 4, 2), LON + LAT)
    cells = P(LAT, LON, None)
    in_specs = (cells, P(LAT, LON), cells, P(), P(), P(), P(), P())
    out_specs = (cells, cells, P(), P(), P())
    return jax.shard_map(shards, mesh=torus, in_specs=in_specs, out_specs=out_specs, check_vma=False)
```

```python
import functools

import jax
import jax.numpy as jnp
from jax import lax
from jax.experimental import pallas as pl
from jax.experimental.pallas import tpu as pltpu
from jax.sharding import Mesh
from jax.sharding import PartitionSpec as P

LINK = jnp.bfloat16
LON = ("x", "yh", "z")
LAT = ("yl", "core")
OUTER = ("x", "yh", "yl", "core")
INNER = ("z",)
ROWS = 32
COLS = 48
C = 128
FF = 256
TERM_ROWS = 576


INSIDE = ((8, 32),)
STRIPS = ((0, 8), (40, 8))
INSIDE_OUT = ((0, 32),)
STRIPS_OUT = ((0, 8), (8, 8))


def fill_rows(pad, own, flags, halo_a, halo_b, first, last, at):
    f32 = jnp.float32
    even = flags[0] == 0
    pad[3 : 3 + ROWS, at : at + last - first, :] = own[:, first:last, :].astype(f32)
    from_a = halo_a[:, first:last, :].astype(f32)
    from_b = halo_b[:, first:last, :].astype(f32)
    pad[0:3, at : at + last - first, :] = jnp.where(even, from_b, from_a)
    pad[3 + ROWS : 6 + ROWS, at : at + last - first, :] = jnp.where(even, from_a, from_b)


def fill_strips(left, right, own, flags, lat_a, lat_b, lon_a, lon_b):
    f32 = jnp.float32
    even = flags[1] == 0
    fill_rows(left, own, flags, lat_a, lat_b, 0, 16, 8)
    fill_rows(right, own, flags, lat_a, lat_b, 32, 48, 0)
    from_a, from_b = lon_a[...].astype(f32), lon_b[...].astype(f32)
    left[:, 5:8, :] = jnp.where(even, from_b, from_a)
    right[:, 16:19, :] = jnp.where(even, from_a, from_b)


def conv_rows(pads, taps, first, step, flip):
    sums = [[jnp.zeros((width, C), jnp.float32) for _, _, width in pads] for _ in range(step)]
    for row in range(step + 6):
        for col in range(7):
            for seg, (pad, start, width) in enumerate(pads):
                cells = pad[first + row, start + col : start + col + width, :]
                for out in range(step):
                    tap = row - out
                    if 0 <= tap < 7:
                        at = tap * 7 + col
                        at = 48 - at if flip else at
                        sums[out][seg] = sums[out][seg] + cells * taps[at : at + 1, :]
    return jnp.concatenate([part for line in sums for part in line], axis=0)


def read_cells(ref, first, step, segs):
    return jnp.concatenate(
        [ref[first + row, c : c + w, :].astype(jnp.float32) for row in range(step) for c, w in segs], axis=0
    )


def write_cells(ref, first, step, segs, values):
    at = 0
    for row in range(step):
        for c, w in segs:
            ref[first + row, c : c + w, :] = values[at : at + w].astype(jnp.bfloat16)
            at += w


def main_rows(step, segs, outs, pads, gmask, params, hidden_out, dz_out, sums, index):
    f32, bf16 = jnp.float32, jnp.bfloat16
    taps, gain, w_in, b_in, w_out = params
    acc_in, acc_out, acc_tap = sums
    first = index * step
    z = conv_rows(pads, taps, first, step, False)
    grad = read_cells(gmask, first, step, segs).astype(bf16)
    average = jnp.mean(z, axis=-1, keepdims=True)
    centre = z - average
    inverse = lax.rsqrt(jnp.mean(centre * centre, axis=-1, keepdims=True) + 1e-06)
    unit = centre * inverse
    normed = (unit * gain[...]).astype(bf16)
    preact = jnp.dot(normed, w_in[...], preferred_element_type=f32) + b_in[...]
    cdf = 0.5 * (1.0 + lax.erf(preact * 0.7071067811865476))
    hidden = (preact * cdf).astype(bf16)
    hidden_out[pl.ds(index * hidden.shape[0], hidden.shape[0]), :] = hidden
    d_hidden = lax.dot_general(grad, w_out[...], (((1,), (1,)), ((), ())), preferred_element_type=f32)
    slopes = cdf + preact * jnp.exp(-0.5 * preact * preact) * 0.3989422804014327
    d_pre = (d_hidden * slopes).astype(bf16)
    contract = (((0,), (0,)), ((), ()))
    acc_out[...] += lax.dot_general(grad, hidden, contract, preferred_element_type=f32)
    acc_in[...] += lax.dot_general(normed, d_pre, contract, preferred_element_type=f32)
    d_norm = lax.dot_general(d_pre, w_in[...], (((1,), (1,)), ((), ())), preferred_element_type=f32)
    scaled = d_norm * gain[...]
    dz = inverse * (
        scaled
        - jnp.mean(scaled, axis=-1, keepdims=True)
        - unit * jnp.mean(scaled * unit, axis=-1, keepdims=True)
    )
    write_cells(dz_out, first, step, outs, dz)
    grads = dz.astype(bf16).astype(f32)
    per_row = sum(w for _, w in segs)
    for tap in range(7):
        for col in range(7):
            total = None
            for row in range(step):
                at = row * per_row
                for pad, start, width in pads:
                    cells = pad[first + row + tap, start + col : start + col + width, :]
                    product = cells * grads[at : at + width]
                    at += width
                    for part in range(0, width, 8):
                        piece = product[part : part + 8]
                        total = piece if total is None else total + piece
            acc_tap[tap * 7 + col] += total


def inside_kernel(
    flags, masked, lat_b, lat_a, gmask, taps, gain, w_in, b_in, w_out,
    hidden, dz_out, acc_in, acc_out, acc_tap, pad,
):
    fill_rows(pad, masked, flags, lat_a, lat_b, 0, COLS, 0)
    for acc in (acc_in, acc_out, acc_tap):
        acc[...] = jnp.zeros_like(acc)
    params = (taps, gain, w_in, b_in, w_out)
    sums = (acc_in, acc_out, acc_tap)

    def block(index, carry):
        main_rows(16, INSIDE, INSIDE_OUT, ((pad, 5, 32),), gmask, params, hidden, dz_out, sums, index)
        return carry

    lax.fori_loop(0, ROWS // 16, block, 0)


def strips_kernel(
    flags, masked, lat_b, lat_a, lon_b, lon_a, gmask, taps, gain, w_in, b_in, w_out,
    had_in, had_out, had_tap,
    hidden, dz_out, terms, left, right, acc_in, acc_out, acc_tap,
):
    fill_strips(left, right, masked, flags, lat_a, lat_b, lon_a, lon_b)
    acc_in[...] = had_in[...]
    acc_out[...] = had_out[...]
    acc_tap[...] = had_tap[...]
    params = (taps, gain, w_in, b_in, w_out)
    pads = ((left, 5, 8), (right, 5, 8))
    main_rows(ROWS, STRIPS, STRIPS_OUT, pads, gmask, params, hidden, dz_out, (acc_in, acc_out, acc_tap), 0)
    half = C // 8
    turned = acc_out[...].T
    tap_sums = jnp.sum(acc_tap[...], axis=1)
    for part in range(half):
        rows = slice(8 * part, 8 * part + 8)
        terms[part, 0:8, :] = acc_in[rows, 0:C].astype(LINK)
        terms[half + part, 0:8, :] = acc_in[rows, C:].astype(LINK)
    for part in range(2 * half):
        terms[2 * half + part, 0:8, :] = turned[8 * part : 8 * part + 8].astype(LINK)
    for part in range(terms.shape[0]):
        row = tap_sums[part : part + 1] if part < 49 else jnp.zeros((1, C), jnp.float32)
        terms[part, 8:9, :] = row.astype(LINK)


def advance_kernel(hidden_in, hidden_st, masked, ocean, w_out, advanced):
    f32 = jnp.float32

    def block(index, carry):
        first = index * 8
        for hidden, segs, outs in ((hidden_in, INSIDE, INSIDE_OUT), (hidden_st, STRIPS, STRIPS_OUT)):
            width = sum(w for _, w in outs)
            size = 8 * width
            out = jnp.dot(hidden[pl.ds(index * size, size), :], w_out[...], preferred_element_type=f32)
            own = read_cells(masked, first, 8, segs)
            keep = read_cells(ocean, first, 8, segs)
            write_cells(advanced, first, 8, segs, own + keep * out)
        return carry

    lax.fori_loop(0, ROWS // 8, block, 0)


def back_kernel(flags, dz_in, dz_st, lon_b, lon_a, lat_b, lat_a, gmask, ocean, taps, field_grad, pad):
    f32 = jnp.float32
    even = flags[1] == 0
    from_a, from_b = lon_a[...].astype(f32), lon_b[...].astype(f32)
    pad[3 : 3 + ROWS, 8:16, :] = dz_st[:, 0:8, :].astype(f32)
    pad[3 : 3 + ROWS, 16:48, :] = dz_in[...].astype(f32)
    pad[3 : 3 + ROWS, 48:56, :] = dz_st[:, 8:16, :].astype(f32)
    pad[3 : 3 + ROWS, 5:8, :] = jnp.where(even, from_b, from_a)
    pad[3 : 3 + ROWS, 8 + COLS : 11 + COLS, :] = jnp.where(even, from_a, from_b)
    even = flags[0] == 0
    from_a, from_b = lat_a[...].astype(f32), lat_b[...].astype(f32)
    pad[0:3, 5 : 11 + COLS, :] = jnp.where(even, from_b, from_a)
    pad[3 + ROWS : 6 + ROWS, 5 : 11 + COLS, :] = jnp.where(even, from_a, from_b)

    def block(index, carry):
        back_rows(4, ((0, COLS),), ((pad, 5, COLS),), gmask, ocean, taps, field_grad, index)
        return carry

    lax.fori_loop(0, ROWS // 4, block, 0)


def back_rows(step, segs, pads, gmask, ocean, taps, field_grad, index):
    first = index * step
    back = conv_rows(pads, taps, first, step, True)
    own = read_cells(gmask, first, step, segs)
    keep = read_cells(ocean, first, step, segs)
    write_cells(field_grad, first, step, segs, own + keep * back)


def final_kernel(parts, kernel_grad, w_in_grad, w_out_grad, *, factor):
    half = C // 8
    for part in range(parts.shape[0]):
        rows = parts[part, 0:8, :].astype(jnp.float32) * factor
        if part < half:
            w_in_grad[8 * part : 8 * part + 8, 0:C] = rows
        elif part < 2 * half:
            w_in_grad[8 * (part - half) : 8 * (part - half) + 8, C:] = rows
        else:
            w_out_grad[8 * (part - 2 * half) : 8 * (part - 2 * half) + 8, :] = rows
    for part in range(49):
        kernel_grad[part // 7, part % 7 : part % 7 + 1, :] = parts[part, 8:9, :].astype(jnp.float32) * factor


def call(body, args, outs, scratch, flops):
    vmem = pl.BlockSpec(memory_space=pltpu.VMEM)
    smem = pl.BlockSpec(memory_space=pltpu.SMEM)
    return pl.pallas_call(
        body,
        out_shape=outs,
        in_specs=[smem if a.dtype == jnp.int32 else vmem for a in args],
        out_specs=[vmem] * len(outs),
        scratch_shapes=scratch,
        compiler_params=pltpu.CompilerParams(vmem_limit_bytes=40 << 20),
        cost_estimate=pl.CostEstimate(flops=flops, bytes_accessed=2 << 20, transcendentals=1 << 19),
    )(*args)


def kind(*shape, dtype=jnp.float32):
    return jax.ShapeDtypeStruct(shape, dtype)


CELLS = kind(ROWS, COLS, C, dtype=jnp.bfloat16)
WIDE = pltpu.VMEM((ROWS + 6, COLS, C), jnp.float32)
PADDED = pltpu.VMEM((ROWS + 6, COLS + 16, C), jnp.float32)
NARROW = pltpu.VMEM((ROWS + 6, 24, C), jnp.float32)
SUMS = ((C, FF), (C, FF), (49, 8, C))


def group_size(axes):
    size = 1
    for axis in axes:
        size *= lax.axis_size(axis)
    return size


def swap(values, axes, count, first, wraps):
    starts = [i for i in range(first, count, 2) if wraps or i + 1 < count]
    pairs = [(i, (i + 1) % count) for i in starts] + [((i + 1) % count, i) for i in starts]
    return lax.ppermute(values, axes, pairs)


def exchange(low, high, axes, count, wraps):
    even = lax.axis_index(axes[-1]) % 2 == 0
    from_b = swap(jnp.where(even, low, high), axes, count, 1, wraps)
    from_a = swap(jnp.where(even, high, low), axes, count, 0, wraps)
    return from_b, from_a


def lat_halo(top, bottom):
    return exchange(top, bottom, LAT, group_size(LAT), False)


def lon_halo(head, tail, lat_b, lat_a):
    even = lax.axis_index(LAT[-1]) % 2 == 0
    north = jnp.where(even, lat_b, lat_a)
    south = jnp.where(even, lat_a, lat_b)
    head = jnp.concatenate([north[:, :3], head, south[:, :3]])
    tail = jnp.concatenate([north[:, COLS - 3 :], tail, south[:, COLS - 3 :]])
    return exchange(head, tail, LON, group_size(LON), True)


def scatter_sum(parts):
    return jnp.sum(lax.all_to_all(parts, OUTER, 0, 0, tiled=True).astype(jnp.float32), axis=0)


def inner_copies(own):
    return jnp.broadcast_to(own[None], (group_size(INNER), *own.shape))


def inner_sum(copies):
    return jnp.sum(lax.all_to_all(copies, INNER, 0, 0, tiled=True), axis=0).astype(LINK)


def hand_out(total):
    spread = jnp.broadcast_to(total[None], (group_size(OUTER), *total.shape))
    return lax.all_to_all(spread, OUTER, 0, 0, tiled=True)


def shards(fields, ocean, cotangent, kernel, ln_gain, w_in, b_in, w_out):
    flags = jnp.stack([lax.axis_index(LAT[-1]) % 2, lax.axis_index(LON[-1]) % 2]).astype(jnp.int32)
    taps = kernel.reshape(49, C)
    params = (taps, ln_gain.reshape(1, C), w_in, b_in.reshape(1, FF), w_out)

    def edge(rows, cols):
        return fields[rows, cols] * ocean[rows, cols].astype(jnp.bfloat16)[..., None]

    every = slice(None)
    lat = lat_halo(edge(slice(0, 3), every), edge(slice(ROWS - 3, ROWS), every))
    ocean_b = jnp.broadcast_to(ocean.astype(jnp.bfloat16)[..., None], fields.shape)
    masked = fields * ocean_b
    gmask = cotangent * ocean_b
    lon = lon_halo(masked[:, :3], masked[:, COLS - 3 :], *lat)
    scratch = [pltpu.VMEM(shape, jnp.float32) for shape in SUMS]
    hidden_in, dz_in, *sums = call(
        inside_kernel,
        (flags, masked, *lat, gmask, *params),
        [
            kind(ROWS * 32, FF, dtype=jnp.bfloat16),
            kind(ROWS, 32, C, dtype=jnp.bfloat16),
            *(kind(*shape) for shape in SUMS),
        ],
        [WIDE],
        350_000_000,
    )
    parts = group_size(OUTER)
    hidden_st, dz_st, terms = call(
        strips_kernel,
        (flags, masked, *lat, *lon, gmask, *params, *sums),
        [
            kind(ROWS * 16, FF, dtype=jnp.bfloat16),
            kind(ROWS, 16, C, dtype=jnp.bfloat16),
            kind(parts, TERM_ROWS // parts, C, dtype=LINK),
        ],
        [NARROW, NARROW, *scratch],
        170_000_000,
    )
    copies = inner_copies(scatter_sum(terms))
    even = flags[1] == 0
    low, high = dz_st[:, :3], dz_st[:, 13:]
    lon_b = swap(jnp.where(even, low, high), LON, group_size(LON), 1, True)
    (advanced,) = call(
        advance_kernel, (hidden_in, hidden_st, masked, ocean_b, w_out), [CELLS], [], 100_000_000
    )
    near = jnp.where(even, high, low)
    lon_a = swap(near, LON, group_size(LON), 0, True)
    lon_a, lon_b, dz_in, advanced, total = lax.optimization_barrier(
        (lon_a, lon_b, dz_in, advanced, inner_sum(copies))
    )
    west, east = jnp.where(even, lon_b, lon_a), jnp.where(even, lon_a, lon_b)

    def full(rows):
        return jnp.concatenate([west[rows], dz_st[rows, :8], dz_in[rows], dz_st[rows, 8:], east[rows]], axis=1)

    lat = exchange(full(slice(0, 3)), full(slice(ROWS - 3, ROWS)), LAT, group_size(LAT), False)
    sums = hand_out(total)
    (field_grad,) = call(
        back_kernel, (flags, dz_in, dz_st, lon_b, lon_a, *lat, gmask, ocean_b, taps), [CELLS], [PADDED], 100_000_000
    )
    cells = ROWS * COLS * group_size(LAT) * group_size(LON)
    kernel_grad, w_in_grad, w_out_grad = call(
        functools.partial(final_kernel, factor=cells**-0.5),
        (sums,),
        [kind(7, 7, C), kind(C, FF), kind(FF, C)],
        [],
        1_000_000,
    )
    return (advanced, field_grad, kernel_grad, w_in_grad, w_out_grad)


def solution(mesh):
    torus = Mesh(mesh.devices.reshape(4, 2, 12, 4, 2), LON + LAT)
    cells = P(LAT, LON, None)
    in_specs = (cells, P(LAT, LON), cells, P(), P(), P(), P(), P())
    out_specs = (cells, cells, P(), P(), P())
    return jax.shard_map(shards, mesh=torus, in_specs=in_specs, out_specs=out_specs, check_vma=False)
```

```python
import functools

import jax
import jax.numpy as jnp
from jax import lax
from jax.experimental import pallas as pl
from jax.experimental.pallas import tpu as pltpu
from jax.sharding import Mesh
from jax.sharding import PartitionSpec as P

LINK = jnp.bfloat16
LON = ("x", "yh", "z")
LAT = ("yl", "core")
OUTER = ("x", "yh", "yl", "core")
INNER = ("z",)
ROWS = 32
COLS = 48
C = 128
FF = 256
TERM_ROWS = 576


INSIDE = ((8, 32),)
STRIPS = ((0, 8), (40, 8))
INSIDE_OUT = ((0, 32),)
STRIPS_OUT = ((0, 8), (8, 8))


def fill_rows(pad, own, flags, halo_a, halo_b, first, last, at):
    f32 = jnp.float32
    even = flags[0] == 0
    pad[3 : 3 + ROWS, at : at + last - first, :] = own[:, first:last, :].astype(f32)
    from_a = halo_a[:, first:last, :].astype(f32)
    from_b = halo_b[:, first:last, :].astype(f32)
    pad[0:3, at : at + last - first, :] = jnp.where(even, from_b, from_a)
    pad[3 + ROWS : 6 + ROWS, at : at + last - first, :] = jnp.where(even, from_a, from_b)


def fill_strips(left, right, own, flags, lat_a, lat_b, lon_a, lon_b):
    f32 = jnp.float32
    even = flags[1] == 0
    fill_rows(left, own, flags, lat_a, lat_b, 0, 16, 8)
    fill_rows(right, own, flags, lat_a, lat_b, 32, 48, 0)
    from_a, from_b = lon_a[...].astype(f32), lon_b[...].astype(f32)
    left[:, 5:8, :] = jnp.where(even, from_b, from_a)
    right[:, 16:19, :] = jnp.where(even, from_a, from_b)


def conv_rows(pads, taps, first, step, flip):
    sums = [[jnp.zeros((width, C), jnp.float32) for _, _, width in pads] for _ in range(step)]
    for row in range(step + 6):
        for col in range(7):
            for seg, (pad, start, width) in enumerate(pads):
                cells = pad[first + row, start + col : start + col + width, :]
                for out in range(step):
                    tap = row - out
                    if 0 <= tap < 7:
                        a, b = (6 - tap, 6 - col) if flip else (tap, col)
                        sums[out][seg] = sums[out][seg] + cells * taps[a, b : b + 1, :]
    return jnp.concatenate([part for line in sums for part in line], axis=0)


def read_cells(ref, first, step, segs):
    return jnp.concatenate(
        [ref[first + row, c : c + w, :].astype(jnp.float32) for row in range(step) for c, w in segs], axis=0
    )


def write_cells(ref, first, step, segs, values):
    at = 0
    for row in range(step):
        for c, w in segs:
            ref[first + row, c : c + w, :] = values[at : at + w].astype(jnp.bfloat16)
            at += w


def main_rows(step, segs, outs, pads, gmask, params, hidden_out, dz_out, sums, index):
    f32, bf16 = jnp.float32, jnp.bfloat16
    taps, vectors, w_in, w_out = params
    gain = vectors[0:1, :]
    b_in = jnp.concatenate([vectors[1:2, :], vectors[2:3, :]], axis=1)
    acc_in, acc_out, acc_tap = sums
    first = index * step
    z = conv_rows(pads, taps, first, step, False)
    grad = read_cells(gmask, first, step, segs).astype(bf16)
    average = jnp.mean(z, axis=-1, keepdims=True)
    centre = z - average
    inverse = lax.rsqrt(jnp.mean(centre * centre, axis=-1, keepdims=True) + 1e-06)
    unit = centre * inverse
    normed = (unit * gain).astype(bf16)
    preact = jnp.dot(normed, w_in[...], preferred_element_type=f32) + b_in
    cdf = 0.5 * (1.0 + lax.erf(preact * 0.7071067811865476))
    hidden = (preact * cdf).astype(bf16)
    hidden_out[pl.ds(index * hidden.shape[0], hidden.shape[0]), :] = hidden
    d_hidden = lax.dot_general(grad, w_out[...], (((1,), (1,)), ((), ())), preferred_element_type=f32)
    slopes = cdf + preact * jnp.exp(-0.5 * preact * preact) * 0.3989422804014327
    d_pre = (d_hidden * slopes).astype(bf16)
    contract = (((0,), (0,)), ((), ()))
    acc_out[...] += lax.dot_general(grad, hidden, contract, preferred_element_type=f32)
    acc_in[...] += lax.dot_general(normed, d_pre, contract, preferred_element_type=f32)
    d_norm = lax.dot_general(d_pre, w_in[...], (((1,), (1,)), ((), ())), preferred_element_type=f32)
    scaled = d_norm * gain
    dz = inverse * (
        scaled
        - jnp.mean(scaled, axis=-1, keepdims=True)
        - unit * jnp.mean(scaled * unit, axis=-1, keepdims=True)
    )
    write_cells(dz_out, first, step, outs, dz)
    grads = dz.astype(bf16).astype(f32)
    per_row = sum(w for _, w in segs)
    for tap in range(7):
        for col in range(7):
            total = None
            for row in range(step):
                at = row * per_row
                for pad, start, width in pads:
                    cells = pad[first + row + tap, start + col : start + col + width, :]
                    product = cells * grads[at : at + width]
                    at += width
                    for part in range(0, width, 8):
                        piece = product[part : part + 8]
                        total = piece if total is None else total + piece
            acc_tap[tap * 7 + col] += total


def inside_kernel(
    flags, masked, lat_b, lat_a, gmask, taps, vectors, w_in, w_out,
    hidden, dz_out, acc_in, acc_out, acc_tap, pad,
):
    fill_rows(pad, masked, flags, lat_a, lat_b, 0, COLS, 0)
    for acc in (acc_in, acc_out, acc_tap):
        acc[...] = jnp.zeros_like(acc)
    params = (taps, vectors, w_in, w_out)
    sums = (acc_in, acc_out, acc_tap)

    def block(index, carry):
        main_rows(16, INSIDE, INSIDE_OUT, ((pad, 5, 32),), gmask, params, hidden, dz_out, sums, index)
        return carry

    lax.fori_loop(0, ROWS // 16, block, 0)


def strips_kernel(
    flags, masked, lat_b, lat_a, lon_b, lon_a, gmask, taps, vectors, w_in, w_out,
    had_in, had_out, had_tap,
    hidden, dz_out, terms, left, right, acc_in, acc_out, acc_tap,
):
    fill_strips(left, right, masked, flags, lat_a, lat_b, lon_a, lon_b)
    acc_in[...] = had_in[...]
    acc_out[...] = had_out[...]
    acc_tap[...] = had_tap[...]
    params = (taps, vectors, w_in, w_out)
    pads = ((left, 5, 8), (right, 5, 8))
    main_rows(ROWS, STRIPS, STRIPS_OUT, pads, gmask, params, hidden, dz_out, (acc_in, acc_out, acc_tap), 0)
    half = C // 8
    turned = acc_out[...].T
    tap_sums = jnp.sum(acc_tap[...], axis=1)
    for part in range(half):
        rows = slice(8 * part, 8 * part + 8)
        terms[part, 0:8, :] = acc_in[rows, 0:C].astype(LINK)
        terms[half + part, 0:8, :] = acc_in[rows, C:].astype(LINK)
    for part in range(2 * half):
        terms[2 * half + part, 0:8, :] = turned[8 * part : 8 * part + 8].astype(LINK)
    for part in range(terms.shape[0]):
        row = tap_sums[part : part + 1] if part < 49 else jnp.zeros((1, C), jnp.float32)
        terms[part, 8:9, :] = row.astype(LINK)


def advance_kernel(hidden_in, hidden_st, masked, ocean, w_out, advanced):
    f32 = jnp.float32

    def block(index, carry):
        first = index * 8
        for hidden, segs, outs in ((hidden_in, INSIDE, INSIDE_OUT), (hidden_st, STRIPS, STRIPS_OUT)):
            width = sum(w for _, w in outs)
            size = 8 * width
            out = jnp.dot(hidden[pl.ds(index * size, size), :], w_out[...], preferred_element_type=f32)
            own = read_cells(masked, first, 8, segs)
            keep = read_cells(ocean, first, 8, segs)
            write_cells(advanced, first, 8, segs, own + keep * out)
        return carry

    lax.fori_loop(0, ROWS // 8, block, 0)


def back_kernel(flags, dz_in, dz_st, lon_b, lon_a, lat_b, lat_a, gmask, ocean, taps, field_grad, pad):
    f32 = jnp.float32
    even = flags[1] == 0
    from_a, from_b = lon_a[...].astype(f32), lon_b[...].astype(f32)
    pad[3 : 3 + ROWS, 8:16, :] = dz_st[:, 0:8, :].astype(f32)
    pad[3 : 3 + ROWS, 16:48, :] = dz_in[...].astype(f32)
    pad[3 : 3 + ROWS, 48:56, :] = dz_st[:, 8:16, :].astype(f32)
    pad[3 : 3 + ROWS, 5:8, :] = jnp.where(even, from_b, from_a)
    pad[3 : 3 + ROWS, 8 + COLS : 11 + COLS, :] = jnp.where(even, from_a, from_b)
    even = flags[0] == 0
    from_a, from_b = lat_a[...].astype(f32), lat_b[...].astype(f32)
    pad[0:3, 5 : 11 + COLS, :] = jnp.where(even, from_b, from_a)
    pad[3 + ROWS : 6 + ROWS, 5 : 11 + COLS, :] = jnp.where(even, from_a, from_b)

    def block(index, carry):
        back_rows(4, ((0, COLS),), ((pad, 5, COLS),), gmask, ocean, taps, field_grad, index)
        return carry

    lax.fori_loop(0, ROWS // 4, block, 0)


def back_rows(step, segs, pads, gmask, ocean, taps, field_grad, index):
    first = index * step
    back = conv_rows(pads, taps, first, step, True)
    own = read_cells(gmask, first, step, segs)
    keep = read_cells(ocean, first, step, segs)
    write_cells(field_grad, first, step, segs, own + keep * back)


def final_kernel(parts, kernel_grad, w_in_grad, w_out_grad, *, factor):
    half = C // 8
    for part in range(parts.shape[0]):
        rows = parts[part, 0:8, :].astype(jnp.float32) * factor
        if part < half:
            w_in_grad[8 * part : 8 * part + 8, 0:C] = rows
        elif part < 2 * half:
            w_in_grad[8 * (part - half) : 8 * (part - half) + 8, C:] = rows
        else:
            w_out_grad[8 * (part - 2 * half) : 8 * (part - 2 * half) + 8, :] = rows
    for part in range(49):
        kernel_grad[part // 7, part % 7 : part % 7 + 1, :] = parts[part, 8:9, :].astype(jnp.float32) * factor


def call(body, args, outs, scratch, flops):
    vmem = pl.BlockSpec(memory_space=pltpu.VMEM)
    smem = pl.BlockSpec(memory_space=pltpu.SMEM)
    return pl.pallas_call(
        body,
        out_shape=outs,
        in_specs=[smem if a.dtype == jnp.int32 else vmem for a in args],
        out_specs=[vmem] * len(outs),
        scratch_shapes=scratch,
        compiler_params=pltpu.CompilerParams(vmem_limit_bytes=40 << 20),
        cost_estimate=pl.CostEstimate(flops=flops, bytes_accessed=2 << 20, transcendentals=1 << 19),
    )(*args)


def kind(*shape, dtype=jnp.float32):
    return jax.ShapeDtypeStruct(shape, dtype)


CELLS = kind(ROWS, COLS, C, dtype=jnp.bfloat16)
WIDE = pltpu.VMEM((ROWS + 6, COLS, C), jnp.float32)
PADDED = pltpu.VMEM((ROWS + 6, COLS + 16, C), jnp.float32)
NARROW = pltpu.VMEM((ROWS + 6, 24, C), jnp.float32)
SUMS = ((C, FF), (C, FF), (49, 8, C))


def group_size(axes):
    size = 1
    for axis in axes:
        size *= lax.axis_size(axis)
    return size


def swap(values, axes, count, first, wraps):
    starts = [i for i in range(first, count, 2) if wraps or i + 1 < count]
    pairs = [(i, (i + 1) % count) for i in starts] + [((i + 1) % count, i) for i in starts]
    return lax.ppermute(values, axes, pairs)


def exchange(low, high, axes, count, wraps):
    even = lax.axis_index(axes[-1]) % 2 == 0
    from_b = swap(jnp.where(even, low, high), axes, count, 1, wraps)
    from_a = swap(jnp.where(even, high, low), axes, count, 0, wraps)
    return from_b, from_a


def lat_halo(top, bottom):
    return exchange(top, bottom, LAT, group_size(LAT), False)


def lon_halo(head, tail, lat_b, lat_a):
    even = lax.axis_index(LAT[-1]) % 2 == 0
    north = jnp.where(even, lat_b, lat_a)
    south = jnp.where(even, lat_a, lat_b)
    head = jnp.concatenate([north[:, :3], head, south[:, :3]])
    tail = jnp.concatenate([north[:, COLS - 3 :], tail, south[:, COLS - 3 :]])
    return exchange(head, tail, LON, group_size(LON), True)


def scatter_sum(parts):
    return jnp.sum(lax.all_to_all(parts, OUTER, 0, 0, tiled=True).astype(jnp.float32), axis=0)


def inner_copies(own):
    return jnp.broadcast_to(own.astype(LINK)[None], (group_size(INNER), *own.shape))


def inner_sum(copies):
    parts = lax.all_to_all(copies, INNER, 0, 0, tiled=True).astype(jnp.float32)
    return jnp.sum(parts, axis=0).astype(LINK)


def hand_out(total):
    spread = jnp.broadcast_to(total[None], (group_size(OUTER), *total.shape))
    return lax.all_to_all(spread, OUTER, 0, 0, tiled=True)


def shards(fields, ocean, cotangent, kernel, ln_gain, w_in, b_in, w_out):
    flags = jnp.stack([lax.axis_index(LAT[-1]) % 2, lax.axis_index(LON[-1]) % 2]).astype(jnp.int32)
    vectors = jnp.concatenate([ln_gain.reshape(1, C), b_in.reshape(2, C)])
    params = (kernel, vectors, w_in, w_out)

    def edge(rows, cols):
        return fields[rows, cols] * ocean[rows, cols].astype(jnp.bfloat16)[..., None]

    every = slice(None)
    lat = lat_halo(edge(slice(0, 3), every), edge(slice(ROWS - 3, ROWS), every))
    ocean_b = jnp.broadcast_to(ocean.astype(jnp.bfloat16)[..., None], fields.shape)
    masked = fields * ocean_b
    gmask = cotangent * ocean_b
    lon = lon_halo(masked[:, :3], masked[:, COLS - 3 :], *lat)
    scratch = [pltpu.VMEM(shape, jnp.float32) for shape in SUMS]
    hidden_in, dz_in, *sums = call(
        inside_kernel,
        (flags, masked, *lat, gmask, *params),
        [
            kind(ROWS * 32, FF, dtype=jnp.bfloat16),
            kind(ROWS, 32, C, dtype=jnp.bfloat16),
            *(kind(*shape) for shape in SUMS),
        ],
        [WIDE],
        350_000_000,
    )
    parts = group_size(OUTER)
    hidden_st, dz_st, terms = call(
        strips_kernel,
        (flags, masked, *lat, *lon, gmask, *params, *sums),
        [
            kind(ROWS * 16, FF, dtype=jnp.bfloat16),
            kind(ROWS, 16, C, dtype=jnp.bfloat16),
            kind(parts, TERM_ROWS // parts, C, dtype=LINK),
        ],
        [NARROW, NARROW, *scratch],
        170_000_000,
    )
    copies = inner_copies(scatter_sum(terms))
    even = flags[1] == 0
    low, high = dz_st[:, :3], dz_st[:, 13:]
    lon_b = swap(jnp.where(even, low, high), LON, group_size(LON), 1, True)
    (advanced,) = call(
        advance_kernel, (hidden_in, hidden_st, masked, ocean_b, w_out), [CELLS], [], 100_000_000
    )
    near = jnp.where(even, high, low)
    lon_a = swap(near, LON, group_size(LON), 0, True)
    lon_a, lon_b, dz_in, advanced, total = lax.optimization_barrier(
        (lon_a, lon_b, dz_in, advanced, inner_sum(copies))
    )
    west, east = jnp.where(even, lon_b, lon_a), jnp.where(even, lon_a, lon_b)

    def full(rows):
        return jnp.concatenate([west[rows], dz_st[rows, :8], dz_in[rows], dz_st[rows, 8:], east[rows]], axis=1)

    lat = exchange(full(slice(0, 3)), full(slice(ROWS - 3, ROWS)), LAT, group_size(LAT), False)
    sums = hand_out(total)
    (field_grad,) = call(
        back_kernel, (flags, dz_in, dz_st, lon_b, lon_a, *lat, gmask, ocean_b, kernel), [CELLS], [PADDED], 100_000_000
    )
    cells = ROWS * COLS * group_size(LAT) * group_size(LON)
    kernel_grad, w_in_grad, w_out_grad = call(
        functools.partial(final_kernel, factor=cells**-0.5),
        (sums,),
        [kind(7, 7, C), kind(C, FF), kind(FF, C)],
        [],
        1_000_000,
    )
    return (advanced, field_grad, kernel_grad, w_in_grad, w_out_grad)


def solution(mesh):
    torus = Mesh(mesh.devices.reshape(4, 2, 12, 4, 2), LON + LAT)
    cells = P(LAT, LON, None)
    in_specs = (cells, P(LAT, LON), cells, P(), P(), P(), P(), P())
    out_specs = (cells, cells, P(), P(), P())
    return jax.shard_map(shards, mesh=torus, in_specs=in_specs, out_specs=out_specs, check_vma=False)
```

```python
import functools

import jax
import jax.numpy as jnp
from jax import lax
from jax.experimental import pallas as pl
from jax.experimental.pallas import tpu as pltpu
from jax.sharding import Mesh
from jax.sharding import PartitionSpec as P

LINK = jnp.bfloat16
LON = ("x", "yh", "z")
LAT = ("yl", "core")
OUTER = ("x", "yh", "yl", "core")
INNER = ("z",)
ROWS = 32
COLS = 48
C = 128
FF = 256


INSIDE = ((8, 32),)
STRIPS = ((0, 8), (40, 8))
INSIDE_OUT = ((0, 32),)
STRIPS_OUT = ((0, 8), (8, 8))


def fill_rows(pad, own, flags, halo_a, halo_b, first, last, at):
    f32 = jnp.float32
    even = flags[0] == 0
    pad[3 : 3 + ROWS, at : at + last - first, :] = own[:, first:last, :].astype(f32)
    from_a = halo_a[:, first:last, :].astype(f32)
    from_b = halo_b[:, first:last, :].astype(f32)
    pad[0:3, at : at + last - first, :] = jnp.where(even, from_b, from_a)
    pad[3 + ROWS : 6 + ROWS, at : at + last - first, :] = jnp.where(even, from_a, from_b)


def fill_strips(left, right, own, flags, lat_a, lat_b, lon_a, lon_b):
    f32 = jnp.float32
    even = flags[1] == 0
    fill_rows(left, own, flags, lat_a, lat_b, 0, 16, 8)
    fill_rows(right, own, flags, lat_a, lat_b, 32, 48, 0)
    from_a, from_b = lon_a[...].astype(f32), lon_b[...].astype(f32)
    left[:, 5:8, :] = jnp.where(even, from_b, from_a)
    right[:, 16:19, :] = jnp.where(even, from_a, from_b)


def conv_rows(pads, taps, first, step, flip):
    sums = [[jnp.zeros((width, C), jnp.float32) for _, _, width in pads] for _ in range(step)]
    for row in range(step + 6):
        for col in range(7):
            for seg, (pad, start, width) in enumerate(pads):
                cells = pad[first + row, start + col : start + col + width, :]
                for out in range(step):
                    tap = row - out
                    if 0 <= tap < 7:
                        a, b = (6 - tap, 6 - col) if flip else (tap, col)
                        sums[out][seg] = sums[out][seg] + cells * taps[a, b : b + 1, :]
    return jnp.concatenate([part for line in sums for part in line], axis=0)


def read_cells(ref, first, step, segs):
    return jnp.concatenate(
        [ref[first + row, c : c + w, :].astype(jnp.float32) for row in range(step) for c, w in segs], axis=0
    )


def write_cells(ref, first, step, segs, values):
    at = 0
    for row in range(step):
        for c, w in segs:
            ref[first + row, c : c + w, :] = values[at : at + w].astype(jnp.bfloat16)
            at += w


def main_rows(step, segs, outs, pads, gmask, params, hidden_out, dz_out, sums, index):
    f32, bf16 = jnp.float32, jnp.bfloat16
    taps, vectors, w_in, w_out = params
    gain = vectors[0:1, :]
    b_in = jnp.concatenate([vectors[1:2, :], vectors[2:3, :]], axis=1)
    acc_in, acc_out, acc_tap = sums
    first = index * step
    z = conv_rows(pads, taps, first, step, False)
    grad = read_cells(gmask, first, step, segs).astype(bf16)
    average = jnp.mean(z, axis=-1, keepdims=True)
    centre = z - average
    inverse = lax.rsqrt(jnp.mean(centre * centre, axis=-1, keepdims=True) + 1e-06)
    unit = centre * inverse
    normed = (unit * gain).astype(bf16)
    preact = jnp.dot(normed, w_in[...], preferred_element_type=f32) + b_in
    cdf = 0.5 * (1.0 + lax.erf(preact * 0.7071067811865476))
    hidden = (preact * cdf).astype(bf16)
    hidden_out[pl.ds(index * hidden.shape[0], hidden.shape[0]), :] = hidden
    d_hidden = lax.dot_general(grad, w_out[...], (((1,), (1,)), ((), ())), preferred_element_type=f32)
    slopes = cdf + preact * jnp.exp(-0.5 * preact * preact) * 0.3989422804014327
    d_pre = (d_hidden * slopes).astype(bf16)
    contract = (((0,), (0,)), ((), ()))
    acc_out[...] += lax.dot_general(grad, hidden, contract, preferred_element_type=f32)
    acc_in[...] += lax.dot_general(normed, d_pre, contract, preferred_element_type=f32)
    d_norm = lax.dot_general(d_pre, w_in[...], (((1,), (1,)), ((), ())), preferred_element_type=f32)
    scaled = d_norm * gain
    dz = inverse * (
        scaled
        - jnp.mean(scaled, axis=-1, keepdims=True)
        - unit * jnp.mean(scaled * unit, axis=-1, keepdims=True)
    )
    write_cells(dz_out, first, step, outs, dz)
    grads = dz.astype(bf16).astype(f32)
    per_row = sum(w for _, w in segs)
    for tap in range(7):
        for col in range(7):
            total = None
            for row in range(step):
                at = row * per_row
                for pad, start, width in pads:
                    cells = pad[first + row + tap, start + col : start + col + width, :]
                    product = cells * grads[at : at + width]
                    at += width
                    for part in range(0, width, 8):
                        piece = product[part : part + 8]
                        total = piece if total is None else total + piece
            acc_tap[tap * 7 + col] += total


def inside_kernel(
    flags, masked, lat_b, lat_a, gmask, taps, vectors, w_in, w_out,
    hidden, dz_out, acc_in, acc_out, acc_tap, pad,
):
    fill_rows(pad, masked, flags, lat_a, lat_b, 0, COLS, 0)
    for acc in (acc_in, acc_out, acc_tap):
        acc[...] = jnp.zeros_like(acc)
    params = (taps, vectors, w_in, w_out)
    sums = (acc_in, acc_out, acc_tap)

    def block(index, carry):
        main_rows(16, INSIDE, INSIDE_OUT, ((pad, 5, 32),), gmask, params, hidden, dz_out, sums, index)
        return carry

    lax.fori_loop(0, ROWS // 16, block, 0)


def strips_kernel(
    flags, masked, lat_b, lat_a, lon_b, lon_a, gmask, taps, vectors, w_in, w_out,
    had_in, had_out, had_tap,
    hidden, dz_out, terms, left, right, acc_in, acc_out, acc_tap, turned,
):
    fill_strips(left, right, masked, flags, lat_a, lat_b, lon_a, lon_b)
    acc_in[...] = had_in[...]
    acc_out[...] = had_out[...]
    acc_tap[...] = had_tap[...]
    params = (taps, vectors, w_in, w_out)
    pads = ((left, 5, 8), (right, 5, 8))
    main_rows(ROWS, STRIPS, STRIPS_OUT, pads, gmask, params, hidden, dz_out, (acc_in, acc_out, acc_tap), 0)
    half = C // 8
    turned[...] = acc_out[...].T
    tap_sums = jnp.sum(acc_tap[...], axis=1)
    for part in range(4 * half):
        if part < 2 * half:
            first, lanes, source = 8 * (part % half), slice(C * (part // half), C * (part // half) + C), acc_in
        else:
            first, lanes, source = 8 * (part - 2 * half), slice(0, C), turned
        row = tap_sums[part : part + 1] if part < 49 else jnp.zeros((1, C), jnp.float32)
        terms[part, 0] = source[first : first + 3, lanes].astype(LINK)
        terms[part, 1] = source[first + 3 : first + 6, lanes].astype(LINK)
        terms[part, 2, 0:2, :] = source[first + 6 : first + 8, lanes].astype(LINK)
        terms[part, 2, 2:3, :] = row.astype(LINK)


def advance_kernel(hidden_in, hidden_st, masked, ocean, w_out, advanced):
    f32 = jnp.float32

    def block(index, carry):
        first = index * 8
        for hidden, segs, outs in ((hidden_in, INSIDE, INSIDE_OUT), (hidden_st, STRIPS, STRIPS_OUT)):
            width = sum(w for _, w in outs)
            size = 8 * width
            out = jnp.dot(hidden[pl.ds(index * size, size), :], w_out[...], preferred_element_type=f32)
            own = read_cells(masked, first, 8, segs)
            keep = read_cells(ocean, first, 8, segs)
            write_cells(advanced, first, 8, segs, own + keep * out)
        return carry

    lax.fori_loop(0, ROWS // 8, block, 0)


def back_kernel(flags, dz_in, dz_st, lon_b, lon_a, lat_b, lat_a, gmask, ocean, taps, field_grad, pad):
    f32 = jnp.float32
    even = flags[1] == 0
    from_a, from_b = lon_a[...].astype(f32), lon_b[...].astype(f32)
    pad[3 : 3 + ROWS, 8:16, :] = dz_st[:, 0:8, :].astype(f32)
    pad[3 : 3 + ROWS, 16:48, :] = dz_in[...].astype(f32)
    pad[3 : 3 + ROWS, 48:56, :] = dz_st[:, 8:16, :].astype(f32)
    pad[3 : 3 + ROWS, 5:8, :] = jnp.where(even, from_b, from_a)
    pad[3 : 3 + ROWS, 8 + COLS : 11 + COLS, :] = jnp.where(even, from_a, from_b)
    even = flags[0] == 0
    from_a, from_b = lat_a[...].astype(f32), lat_b[...].astype(f32)
    pad[0:3, 5 : 11 + COLS, :] = jnp.where(even, from_b, from_a)
    pad[3 + ROWS : 6 + ROWS, 5 : 11 + COLS, :] = jnp.where(even, from_a, from_b)

    def block(index, carry):
        back_rows(4, ((0, COLS),), ((pad, 5, COLS),), gmask, ocean, taps, field_grad, index)
        return carry

    lax.fori_loop(0, ROWS // 4, block, 0)


def back_rows(step, segs, pads, gmask, ocean, taps, field_grad, index):
    first = index * step
    back = conv_rows(pads, taps, first, step, True)
    own = read_cells(gmask, first, step, segs)
    keep = read_cells(ocean, first, step, segs)
    write_cells(field_grad, first, step, segs, own + keep * back)


def final_kernel(parts, kernel_grad, w_in_grad, w_out_grad, *, factor):
    half = C // 8
    for part in range(4 * half):
        if part < 2 * half:
            first, lanes, target = 8 * (part % half), slice(C * (part // half), C * (part // half) + C), w_in_grad
        else:
            first, lanes, target = 8 * (part - 2 * half), slice(0, C), w_out_grad
        target[first : first + 3, lanes] = parts[part, 0].astype(jnp.float32) * factor
        target[first + 3 : first + 6, lanes] = parts[part, 1].astype(jnp.float32) * factor
        target[first + 6 : first + 8, lanes] = parts[part, 2, 0:2, :].astype(jnp.float32) * factor
    for part in range(49):
        kernel_grad[part // 7, part % 7 : part % 7 + 1, :] = parts[part, 2, 2:3, :].astype(jnp.float32) * factor


def call(body, args, outs, scratch, flops):
    vmem = pl.BlockSpec(memory_space=pltpu.VMEM)
    smem = pl.BlockSpec(memory_space=pltpu.SMEM)
    return pl.pallas_call(
        body,
        out_shape=outs,
        in_specs=[smem if a.dtype == jnp.int32 else vmem for a in args],
        out_specs=[vmem] * len(outs),
        scratch_shapes=scratch,
        compiler_params=pltpu.CompilerParams(vmem_limit_bytes=40 << 20),
        cost_estimate=pl.CostEstimate(flops=flops, bytes_accessed=2 << 20, transcendentals=1 << 19),
    )(*args)


def kind(*shape, dtype=jnp.float32):
    return jax.ShapeDtypeStruct(shape, dtype)


CELLS = kind(ROWS, COLS, C, dtype=jnp.bfloat16)
WIDE = pltpu.VMEM((ROWS + 6, COLS, C), jnp.float32)
PADDED = pltpu.VMEM((ROWS + 6, COLS + 16, C), jnp.float32)
NARROW = pltpu.VMEM((ROWS + 6, 24, C), jnp.float32)
SUMS = ((C, FF), (C, FF), (49, 8, C))


def group_size(axes):
    size = 1
    for axis in axes:
        size *= lax.axis_size(axis)
    return size


def swap(values, axes, count, first, wraps):
    starts = [i for i in range(first, count, 2) if wraps or i + 1 < count]
    pairs = [(i, (i + 1) % count) for i in starts] + [((i + 1) % count, i) for i in starts]
    return lax.ppermute(values, axes, pairs)


def exchange(low, high, axes, count, wraps):
    even = lax.axis_index(axes[-1]) % 2 == 0
    from_b = swap(jnp.where(even, low, high), axes, count, 1, wraps)
    from_a = swap(jnp.where(even, high, low), axes, count, 0, wraps)
    return from_b, from_a


def lat_halo(top, bottom):
    return exchange(top, bottom, LAT, group_size(LAT), False)


def lon_halo(head, tail, lat_b, lat_a):
    even = lax.axis_index(LAT[-1]) % 2 == 0
    north = jnp.where(even, lat_b, lat_a)
    south = jnp.where(even, lat_a, lat_b)
    head = jnp.concatenate([north[:, :3], head, south[:, :3]])
    tail = jnp.concatenate([north[:, COLS - 3 :], tail, south[:, COLS - 3 :]])
    return exchange(head, tail, LON, group_size(LON), True)


def scatter_sum(parts):
    return jnp.sum(lax.all_to_all(parts, OUTER, 0, 0, tiled=True).astype(jnp.float32), axis=0)


def inner_copies(own):
    return jnp.broadcast_to(own.astype(LINK)[None], (group_size(INNER), *own.shape))


def inner_sum(copies):
    parts = lax.all_to_all(copies, INNER, 0, 0, tiled=True).astype(jnp.float32)
    return jnp.sum(parts, axis=0).astype(LINK)


def hand_out(total):
    spread = jnp.broadcast_to(total[None], (group_size(OUTER), *total.shape))
    return lax.all_to_all(spread, OUTER, 0, 0, tiled=True)


def shards(fields, ocean, cotangent, kernel, ln_gain, w_in, b_in, w_out):
    flags = jnp.stack([lax.axis_index(LAT[-1]) % 2, lax.axis_index(LON[-1]) % 2]).astype(jnp.int32)
    vectors = jnp.concatenate([ln_gain.reshape(1, C), b_in.reshape(2, C)])
    params = (kernel, vectors, w_in, w_out)

    def edge(rows, cols):
        return fields[rows, cols] * ocean[rows, cols].astype(jnp.bfloat16)[..., None]

    every = slice(None)
    lat = lat_halo(edge(slice(0, 3), every), edge(slice(ROWS - 3, ROWS), every))
    ocean_b = jnp.broadcast_to(ocean.astype(jnp.bfloat16)[..., None], fields.shape)
    masked = fields * ocean_b
    gmask = cotangent * ocean_b
    lon = lon_halo(masked[:, :3], masked[:, COLS - 3 :], *lat)
    scratch = [pltpu.VMEM(shape, jnp.float32) for shape in SUMS]
    hidden_in, dz_in, *sums = call(
        inside_kernel,
        (flags, masked, *lat, gmask, *params),
        [
            kind(ROWS * 32, FF, dtype=jnp.bfloat16),
            kind(ROWS, 32, C, dtype=jnp.bfloat16),
            *(kind(*shape) for shape in SUMS),
        ],
        [WIDE],
        350_000_000,
    )
    parts = group_size(OUTER)
    hidden_st, dz_st, terms = call(
        strips_kernel,
        (flags, masked, *lat, *lon, gmask, *params, *sums),
        [
            kind(ROWS * 16, FF, dtype=jnp.bfloat16),
            kind(ROWS, 16, C, dtype=jnp.bfloat16),
            kind(parts, 3, 3, C, dtype=LINK),
        ],
        [NARROW, NARROW, *scratch, pltpu.VMEM((FF, C), jnp.float32)],
        170_000_000,
    )
    copies = inner_copies(scatter_sum(terms))
    even = flags[1] == 0
    low, high = dz_st[:, :3], dz_st[:, 13:]
    lon_b = swap(jnp.where(even, low, high), LON, group_size(LON), 1, True)
    (advanced,) = call(
        advance_kernel, (hidden_in, hidden_st, masked, ocean_b, w_out), [CELLS], [], 100_000_000
    )
    near = jnp.where(even, high, low)
    lon_a = swap(near, LON, group_size(LON), 0, True)
    lon_b, lon_a, dz_in, advanced, total = lax.optimization_barrier(
        (lon_b, lon_a, dz_in, advanced, inner_sum(copies))
    )
    west, east = jnp.where(even, lon_b, lon_a), jnp.where(even, lon_a, lon_b)

    def full(rows):
        return jnp.concatenate([west[rows], dz_st[rows, :8], dz_in[rows], dz_st[rows, 8:], east[rows]], axis=1)

    lat = exchange(full(slice(0, 3)), full(slice(ROWS - 3, ROWS)), LAT, group_size(LAT), False)
    sums = hand_out(total)
    (field_grad,) = call(
        back_kernel, (flags, dz_in, dz_st, lon_b, lon_a, *lat, gmask, ocean_b, kernel), [CELLS], [PADDED], 100_000_000
    )
    cells = ROWS * COLS * group_size(LAT) * group_size(LON)
    kernel_grad, w_in_grad, w_out_grad = call(
        functools.partial(final_kernel, factor=cells**-0.5),
        (sums,),
        [kind(7, 7, C), kind(C, FF), kind(FF, C)],
        [],
        1_000_000,
    )
    return (advanced, field_grad, kernel_grad, w_in_grad, w_out_grad)


def solution(mesh):
    torus = Mesh(mesh.devices.reshape(4, 2, 12, 4, 2), LON + LAT)
    cells = P(LAT, LON, None)
    in_specs = (cells, P(LAT, LON), cells, P(), P(), P(), P(), P())
    out_specs = (cells, cells, P(), P(), P())
    return jax.shard_map(shards, mesh=torus, in_specs=in_specs, out_specs=out_specs, check_vma=False)
```

```python
import functools

import jax
import jax.numpy as jnp
from jax import lax
from jax.experimental import pallas as pl
from jax.experimental.pallas import tpu as pltpu
from jax.sharding import Mesh
from jax.sharding import PartitionSpec as P

LINK = jnp.bfloat16
LON = ("x", "yh", "z")
LAT = ("yl", "core")
OUTER = ("x", "yh", "yl", "core")
INNER = ("z",)
ROWS = 32
COLS = 48
C = 128
FF = 256


INSIDE = ((8, 32),)
STRIPS = ((0, 8), (40, 8))
INSIDE_OUT = ((0, 32),)
STRIPS_OUT = ((0, 8), (8, 8))


def fill_rows(pad, own, flags, halo_a, halo_b, first, last, at):
    f32 = jnp.float32
    even = flags[0] == 0
    pad[3 : 3 + ROWS, at : at + last - first, :] = own[:, first:last, :].astype(f32)
    from_a = halo_a[:, first:last, :].astype(f32)
    from_b = halo_b[:, first:last, :].astype(f32)
    pad[0:3, at : at + last - first, :] = jnp.where(even, from_b, from_a)
    pad[3 + ROWS : 6 + ROWS, at : at + last - first, :] = jnp.where(even, from_a, from_b)


def fill_strips(left, right, own, flags, lat_a, lat_b, lon_a, lon_b):
    f32 = jnp.float32
    even = flags[1] == 0
    fill_rows(left, own, flags, lat_a, lat_b, 0, 16, 8)
    fill_rows(right, own, flags, lat_a, lat_b, 32, 48, 0)
    from_a, from_b = lon_a[...].astype(f32), lon_b[...].astype(f32)
    left[:, 5:8, :] = jnp.where(even, from_b, from_a)
    right[:, 16:19, :] = jnp.where(even, from_a, from_b)


def conv_rows(pads, taps, first, step, flip):
    sums = [[jnp.zeros((width, C), jnp.float32) for _, _, width in pads] for _ in range(step)]
    for row in range(step + 6):
        for col in range(7):
            for seg, (pad, start, width) in enumerate(pads):
                cells = pad[first + row, start + col : start + col + width, :]
                for out in range(step):
                    tap = row - out
                    if 0 <= tap < 7:
                        a, b = (6 - tap, 6 - col) if flip else (tap, col)
                        sums[out][seg] = sums[out][seg] + cells * taps[a, b : b + 1, :]
    return jnp.concatenate([part for line in sums for part in line], axis=0)


def read_cells(ref, first, step, segs):
    return jnp.concatenate(
        [ref[first + row, c : c + w, :].astype(jnp.float32) for row in range(step) for c, w in segs], axis=0
    )


def write_cells(ref, first, step, segs, values):
    at = 0
    for row in range(step):
        for c, w in segs:
            ref[first + row, c : c + w, :] = values[at : at + w].astype(jnp.bfloat16)
            at += w


def main_rows(step, segs, outs, pads, gmask, params, hidden_out, dz_out, sums, index):
    f32, bf16 = jnp.float32, jnp.bfloat16
    taps, vectors, w_in, w_out = params
    gain = vectors[0:1, :]
    b_in = jnp.concatenate([vectors[1:2, :], vectors[2:3, :]], axis=1)
    acc_in, acc_out, acc_tap = sums
    first = index * step
    z = conv_rows(pads, taps, first, step, False)
    grad = read_cells(gmask, first, step, segs).astype(bf16)
    average = jnp.mean(z, axis=-1, keepdims=True)
    centre = z - average
    inverse = lax.rsqrt(jnp.mean(centre * centre, axis=-1, keepdims=True) + 1e-06)
    unit = centre * inverse
    normed = (unit * gain).astype(bf16)
    preact = jnp.dot(normed, w_in[...], preferred_element_type=f32) + b_in
    cdf = 0.5 * (1.0 + lax.erf(preact * 0.7071067811865476))
    hidden = (preact * cdf).astype(bf16)
    hidden_out[pl.ds(index * hidden.shape[0], hidden.shape[0]), :] = hidden
    d_hidden = lax.dot_general(grad, w_out[...], (((1,), (1,)), ((), ())), preferred_element_type=f32)
    slopes = cdf + preact * jnp.exp(-0.5 * preact * preact) * 0.3989422804014327
    d_pre = (d_hidden * slopes).astype(bf16)
    contract = (((0,), (0,)), ((), ()))
    acc_out[...] += lax.dot_general(grad, hidden, contract, preferred_element_type=f32)
    acc_in[...] += lax.dot_general(normed, d_pre, contract, preferred_element_type=f32)
    d_norm = lax.dot_general(d_pre, w_in[...], (((1,), (1,)), ((), ())), preferred_element_type=f32)
    scaled = d_norm * gain
    dz = inverse * (
        scaled
        - jnp.mean(scaled, axis=-1, keepdims=True)
        - unit * jnp.mean(scaled * unit, axis=-1, keepdims=True)
    )
    write_cells(dz_out, first, step, outs, dz)
    grads = dz.astype(bf16).astype(f32)
    per_row = sum(w for _, w in segs)
    for tap in range(7):
        for col in range(7):
            total = None
            for row in range(step):
                at = row * per_row
                for pad, start, width in pads:
                    cells = pad[first + row + tap, start + col : start + col + width, :]
                    product = cells * grads[at : at + width]
                    at += width
                    for part in range(0, width, 8):
                        piece = product[part : part + 8]
                        total = piece if total is None else total + piece
            acc_tap[tap * 7 + col] += total


def inside_kernel(
    flags, masked, lat_b, lat_a, gmask, taps, vectors, w_in, w_out,
    hidden, dz_out, acc_in, acc_out, acc_tap, pad,
):
    fill_rows(pad, masked, flags, lat_a, lat_b, 0, COLS, 0)
    for acc in (acc_in, acc_out, acc_tap):
        acc[...] = jnp.zeros_like(acc)
    params = (taps, vectors, w_in, w_out)
    sums = (acc_in, acc_out, acc_tap)

    def block(index, carry):
        main_rows(16, INSIDE, INSIDE_OUT, ((pad, 5, 32),), gmask, params, hidden, dz_out, sums, index)
        return carry

    lax.fori_loop(0, ROWS // 16, block, 0)


def strips_kernel(
    flags, masked, lat_b, lat_a, lon_b, lon_a, gmask, taps, vectors, w_in, w_out,
    had_in, had_out, had_tap,
    hidden, dz_out, terms, left, right, acc_in, acc_out, acc_tap, turned,
):
    fill_strips(left, right, masked, flags, lat_a, lat_b, lon_a, lon_b)
    acc_in[...] = had_in[...]
    acc_out[...] = had_out[...]
    acc_tap[...] = had_tap[...]
    params = (taps, vectors, w_in, w_out)
    pads = ((left, 5, 8), (right, 5, 8))
    main_rows(ROWS, STRIPS, STRIPS_OUT, pads, gmask, params, hidden, dz_out, (acc_in, acc_out, acc_tap), 0)
    half = C // 8
    turned[...] = acc_out[...].T
    tap_sums = jnp.sum(acc_tap[...], axis=1)
    for part in range(4 * half):
        if part < 2 * half:
            first, lanes, source = 8 * (part % half), slice(C * (part // half), C * (part // half) + C), acc_in
        else:
            first, lanes, source = 8 * (part - 2 * half), slice(0, C), turned
        row = tap_sums[part : part + 1] if part < 49 else jnp.zeros((1, C), jnp.float32)
        terms[part, 0] = source[first : first + 3, lanes].astype(LINK)
        terms[part, 1] = source[first + 3 : first + 6, lanes].astype(LINK)
        terms[part, 2, 0:2, :] = source[first + 6 : first + 8, lanes].astype(LINK)
        terms[part, 2, 2:3, :] = row.astype(LINK)


def advance_kernel(hidden_in, hidden_st, masked, ocean, w_out, advanced):
    f32 = jnp.float32

    def block(index, carry):
        first = index * 8
        for hidden, segs, outs in ((hidden_in, INSIDE, INSIDE_OUT), (hidden_st, STRIPS, STRIPS_OUT)):
            width = sum(w for _, w in outs)
            size = 8 * width
            out = jnp.dot(hidden[pl.ds(index * size, size), :], w_out[...], preferred_element_type=f32)
            own = read_cells(masked, first, 8, segs)
            keep = read_cells(ocean, first, 8, segs)
            write_cells(advanced, first, 8, segs, own + keep * out)
        return carry

    lax.fori_loop(0, ROWS // 8, block, 0)


def back_inside_kernel(dz_in, dz_st, gmask, ocean, taps, part, pad):
    f32 = jnp.float32
    pad[:, 0:8, :] = dz_st[:, 0:8, :].astype(f32)
    pad[:, 8:40, :] = dz_in[...].astype(f32)
    pad[:, 40:48, :] = dz_st[:, 8:16, :].astype(f32)

    def block(index, carry):
        back = conv_rows(((pad, 5, 32),), taps, 4 * index + 1, 4, True)
        own = read_cells(gmask, 4 * index + 4, 4, INSIDE)
        keep = read_cells(ocean, 4 * index + 4, 4, INSIDE)
        write_cells(part, 4 * index, 4, INSIDE_OUT, own + keep * back)
        return carry

    lax.fori_loop(0, 6, block, 0)


def back_kernel(flags, dz_in, dz_st, lon_b, lon_a, lat_b, lat_a, gmask, ocean, taps, part, field_grad, pad):
    f32 = jnp.float32
    even = flags[1] == 0
    from_a, from_b = lon_a[...].astype(f32), lon_b[...].astype(f32)
    pad[3 : 3 + ROWS, 8:16, :] = dz_st[:, 0:8, :].astype(f32)
    pad[3 : 3 + ROWS, 16:48, :] = dz_in[...].astype(f32)
    pad[3 : 3 + ROWS, 48:56, :] = dz_st[:, 8:16, :].astype(f32)
    pad[3 : 3 + ROWS, 5:8, :] = jnp.where(even, from_b, from_a)
    pad[3 : 3 + ROWS, 8 + COLS : 11 + COLS, :] = jnp.where(even, from_a, from_b)
    even = flags[0] == 0
    from_a, from_b = lat_a[...].astype(f32), lat_b[...].astype(f32)
    pad[0:3, 5 : 11 + COLS, :] = jnp.where(even, from_b, from_a)
    pad[3 + ROWS : 6 + ROWS, 5 : 11 + COLS, :] = jnp.where(even, from_a, from_b)

    def ends(index, carry):
        back_rows(4, 28 * index, ((0, COLS),), ((pad, 5, COLS),), gmask, ocean, taps, field_grad)
        return carry

    def sides(index, carry):
        back_rows(8, 8 * index + 4, STRIPS, ((pad, 5, 8), (pad, 45, 8)), gmask, ocean, taps, field_grad)
        return carry

    field_grad[4:28, 8:40, :] = part[...]
    lax.fori_loop(0, 2, ends, 0)
    lax.fori_loop(0, 3, sides, 0)


def back_rows(step, first, segs, pads, gmask, ocean, taps, field_grad):
    back = conv_rows(pads, taps, first, step, True)
    own = read_cells(gmask, first, step, segs)
    keep = read_cells(ocean, first, step, segs)
    write_cells(field_grad, first, step, segs, own + keep * back)


def final_kernel(parts, kernel_grad, w_in_grad, w_out_grad, *, factor):
    half = C // 8
    for part in range(4 * half):
        if part < 2 * half:
            first, lanes, target = 8 * (part % half), slice(C * (part // half), C * (part // half) + C), w_in_grad
        else:
            first, lanes, target = 8 * (part - 2 * half), slice(0, C), w_out_grad
        target[first : first + 3, lanes] = parts[part, 0].astype(jnp.float32) * factor
        target[first + 3 : first + 6, lanes] = parts[part, 1].astype(jnp.float32) * factor
        target[first + 6 : first + 8, lanes] = parts[part, 2, 0:2, :].astype(jnp.float32) * factor
    for part in range(49):
        kernel_grad[part // 7, part % 7 : part % 7 + 1, :] = parts[part, 2, 2:3, :].astype(jnp.float32) * factor


def call(body, args, outs, scratch, flops):
    vmem = pl.BlockSpec(memory_space=pltpu.VMEM)
    smem = pl.BlockSpec(memory_space=pltpu.SMEM)
    return pl.pallas_call(
        body,
        out_shape=outs,
        in_specs=[smem if a.dtype == jnp.int32 else vmem for a in args],
        out_specs=[vmem] * len(outs),
        scratch_shapes=scratch,
        compiler_params=pltpu.CompilerParams(vmem_limit_bytes=40 << 20),
        cost_estimate=pl.CostEstimate(flops=flops, bytes_accessed=2 << 20, transcendentals=1 << 19),
    )(*args)


def kind(*shape, dtype=jnp.float32):
    return jax.ShapeDtypeStruct(shape, dtype)


CELLS = kind(ROWS, COLS, C, dtype=jnp.bfloat16)
WIDE = pltpu.VMEM((ROWS + 6, COLS, C), jnp.float32)
PADDED = pltpu.VMEM((ROWS + 6, COLS + 16, C), jnp.float32)
NARROW = pltpu.VMEM((ROWS + 6, 24, C), jnp.float32)
SUMS = ((C, FF), (C, FF), (49, 8, C))


def group_size(axes):
    size = 1
    for axis in axes:
        size *= lax.axis_size(axis)
    return size


def swap(values, axes, count, first, wraps):
    starts = [i for i in range(first, count, 2) if wraps or i + 1 < count]
    pairs = [(i, (i + 1) % count) for i in starts] + [((i + 1) % count, i) for i in starts]
    return lax.ppermute(values, axes, pairs)


def exchange(low, high, axes, count, wraps):
    even = lax.axis_index(axes[-1]) % 2 == 0
    from_b = swap(jnp.where(even, low, high), axes, count, 1, wraps)
    from_a = swap(jnp.where(even, high, low), axes, count, 0, wraps)
    return from_b, from_a


def lat_halo(top, bottom):
    return exchange(top, bottom, LAT, group_size(LAT), False)


def lon_halo(head, tail, lat_b, lat_a):
    even = lax.axis_index(LAT[-1]) % 2 == 0
    north = jnp.where(even, lat_b, lat_a)
    south = jnp.where(even, lat_a, lat_b)
    head = jnp.concatenate([north[:, :3], head, south[:, :3]])
    tail = jnp.concatenate([north[:, COLS - 3 :], tail, south[:, COLS - 3 :]])
    return exchange(head, tail, LON, group_size(LON), True)


def scatter_sum(parts):
    return jnp.sum(lax.all_to_all(parts, OUTER, 0, 0, tiled=True).astype(jnp.float32), axis=0)


def inner_copies(own):
    return jnp.broadcast_to(own.astype(LINK)[None], (group_size(INNER), *own.shape))


def inner_sum(copies):
    parts = lax.all_to_all(copies, INNER, 0, 0, tiled=True).astype(jnp.float32)
    return jnp.sum(parts, axis=0).astype(LINK)


def hand_out(total):
    spread = jnp.broadcast_to(total[None], (group_size(OUTER), *total.shape))
    return lax.all_to_all(spread, OUTER, 0, 0, tiled=True)


def shards(fields, ocean, cotangent, kernel, ln_gain, w_in, b_in, w_out):
    flags = jnp.stack([lax.axis_index(LAT[-1]) % 2, lax.axis_index(LON[-1]) % 2]).astype(jnp.int32)
    vectors = jnp.concatenate([ln_gain.reshape(1, C), b_in.reshape(2, C)])
    params = (kernel, vectors, w_in, w_out)

    def edge(rows, cols):
        return fields[rows, cols] * ocean[rows, cols].astype(jnp.bfloat16)[..., None]

    every = slice(None)
    lat = lat_halo(edge(slice(0, 3), every), edge(slice(ROWS - 3, ROWS), every))
    ocean_b = jnp.broadcast_to(ocean.astype(jnp.bfloat16)[..., None], fields.shape)
    masked = fields * ocean_b
    gmask = cotangent * ocean_b
    lon = lon_halo(masked[:, :3], masked[:, COLS - 3 :], *lat)
    scratch = [pltpu.VMEM(shape, jnp.float32) for shape in SUMS]
    hidden_in, dz_in, *sums = call(
        inside_kernel,
        (flags, masked, *lat, gmask, *params),
        [
            kind(ROWS * 32, FF, dtype=jnp.bfloat16),
            kind(ROWS, 32, C, dtype=jnp.bfloat16),
            *(kind(*shape) for shape in SUMS),
        ],
        [WIDE],
        350_000_000,
    )
    parts = group_size(OUTER)
    hidden_st, dz_st, terms = call(
        strips_kernel,
        (flags, masked, *lat, *lon, gmask, *params, *sums),
        [
            kind(ROWS * 16, FF, dtype=jnp.bfloat16),
            kind(ROWS, 16, C, dtype=jnp.bfloat16),
            kind(parts, 3, 3, C, dtype=LINK),
        ],
        [NARROW, NARROW, *scratch, pltpu.VMEM((FF, C), jnp.float32)],
        170_000_000,
    )
    copies = inner_copies(scatter_sum(terms))
    even = flags[1] == 0
    low, high = dz_st[:, :3], dz_st[:, 13:]
    lon_b = swap(jnp.where(even, low, high), LON, group_size(LON), 1, True)
    (advanced,) = call(
        advance_kernel, (hidden_in, hidden_st, masked, ocean_b, w_out), [CELLS], [], 100_000_000
    )
    near = jnp.where(even, high, low)
    lon_a = swap(near, LON, group_size(LON), 0, True)
    (part,) = call(
        back_inside_kernel,
        (dz_in, dz_st, gmask, ocean_b, kernel),
        [kind(24, 32, C, dtype=jnp.bfloat16)],
        [pltpu.VMEM((ROWS, COLS, C), jnp.float32)],
        50_000_000,
    )
    lon_b, lon_a, dz_in, advanced, part, total = lax.optimization_barrier(
        (lon_b, lon_a, dz_in, advanced, part, inner_sum(copies))
    )
    west, east = jnp.where(even, lon_b, lon_a), jnp.where(even, lon_a, lon_b)

    def full(rows):
        return jnp.concatenate([west[rows], dz_st[rows, :8], dz_in[rows], dz_st[rows, 8:], east[rows]], axis=1)

    lat = exchange(full(slice(0, 3)), full(slice(ROWS - 3, ROWS)), LAT, group_size(LAT), False)
    sums = hand_out(total)
    (field_grad,) = call(
        back_kernel, (flags, dz_in, dz_st, lon_b, lon_a, *lat, gmask, ocean_b, kernel, part), [CELLS], [PADDED], 50_000_000
    )
    cells = ROWS * COLS * group_size(LAT) * group_size(LON)
    kernel_grad, w_in_grad, w_out_grad = call(
        functools.partial(final_kernel, factor=cells**-0.5),
        (sums,),
        [kind(7, 7, C), kind(C, FF), kind(FF, C)],
        [],
        1_000_000,
    )
    return (advanced, field_grad, kernel_grad, w_in_grad, w_out_grad)


def solution(mesh):
    torus = Mesh(mesh.devices.reshape(4, 2, 12, 4, 2), LON + LAT)
    cells = P(LAT, LON, None)
    in_specs = (cells, P(LAT, LON), cells, P(), P(), P(), P(), P())
    out_specs = (cells, cells, P(), P(), P())
    return jax.shard_map(shards, mesh=torus, in_specs=in_specs, out_specs=out_specs, check_vma=False)
```
